32 devices in a mesh: dp: 8 (over z, y), mp: 4 (over x, core).
Axes of the slice: x: 2, y: 2, z: 4, core: 2. Of those that a mesh axis runs over, the one named last changes fastest.
Arguments:
- h_in: float32 [4096, 768], P(('dp', 'mp')), may hold values from -6 to 6
- w_z: bfloat16 [2, 768, 1536], P(None, 'dp', 'mp'), may hold values from -0.21875 to 0.21875
- w_x: bfloat16 [2, 768, 1536], P(None, 'dp', 'mp'), may hold values from -0.21875 to 0.21875
- w_bc: bfloat16 [2, 768, 256], P(None, ('dp', 'mp')), may hold values from -0.21875 to 0.21875
- w_dt: bfloat16 [2, 768, 24], P(None, 'dp', 'mp'), may hold values from -0.21875 to 0.21875
- w_out: bfloat16 [2, 1536, 768], P(None, 'mp', 'dp'), may hold values from -0.15625 to 0.15625
- conv_x: float32 [2, 5, 1536], P(None, None, 'mp'), may hold values from -0.5 to 0.5
- conv_bc: bfloat16 [2, 5, 256], P(None, None, ('dp', 'mp')), may hold values from -0.5 to 0.5
- dt_bias: float32 [2, 24], P(None, 'mp'), may hold values from -6 to -2
- a_log: float32 [2, 24], P(None, 'mp'), may hold values from 0 to 2.8
- d_skip: float32 [2, 24], P(None, 'mp'), may hold values from 0.5 to 1.5
- rms_gain: bfloat16 [2, 768], P(None, ('dp', 'mp')), may hold values from 0.5 to 1.5
- gnorm_gain: float32 [2, 1536], P(None, 'mp'), may hold values from 0.5 to 1.5
- seg_ids: int32 [8, 512], P('dp'), may hold values from 0 to 7, never falling along the last dimension, each value on 1 to 256 neighbouring positions
- cotangent: float32 [4096, 768], P(('dp', 'mp')), may hold values from -6 to 6
Outputs:
- h_out: float32 [4096, 768], P(('dp', 'mp'))
- dh_in: float32 [4096, 768], P(('dp', 'mp'))
- grad_w_z: float32 [2, 768, 1536], P(None, 'dp', 'mp')
- grad_w_x: float32 [2, 768, 1536], P(None, 'dp', 'mp')
- grad_w_bc: float32 [2, 768, 256], P(None, ('dp', 'mp'))
- grad_w_dt: float32 [2, 768, 24], P(None, 'dp', 'mp')
- grad_w_out: float32 [2, 1536, 768], P(None, 'mp', 'dp')
- grad_conv_x: float32 [2, 5, 1536], P(None, None, 'mp')
- grad_conv_bc: float32 [2, 5, 256], P(None, None, ('dp', 'mp'))
- grad_dt_bias: float32 [2, 24], P(None, 'mp')
- grad_a_log: float32 [2, 24], P(None, 'mp')
- grad_d_skip: float32 [2, 24], P(None, 'mp')
- grad_rms_gain: float32 [2, 768], P(None, ('dp', 'mp'))
- grad_gnorm_gain: float32 [2, 1536], P(None, 'mp')
The draws below stay inside these ranges and needn't reach their ends.
Inputs may be any that keep to these rules, and one draw needn't show every extreme that they name: `seg_ids`: along each sequence the document numbers never fall; a document spans 1 to 256 tokens, and one spans exactly 256.
All inputs are finite; a program needn't handle non-finite values.
Results may differ from the reference program's by a relative error of at most 0.015.
Values may be sent and summed in bfloat16 or wider, within the bound.
No kernel may reach another device: no remote copies, remote signals or barrier semaphores. Data moves between devices by JAX's collectives and lax.ppermute only.
A program may use at most 128 MiB of HBM per device.

```python
import math
from functools import partial
import jax
import jax.numpy as jnp
import numpy as np
from jax import lax

D = 768
HEADS = 24
NSTATE = 128
CONV = 4
GROUP = 128
LAYERS = 2
SEQ = 512
INNER = 1536
SEQS = 8
TOKENS = 4096


def block_levels(own_key, extent, split, least, top_value):
    factor_of = 1.0
    for axis_at, shards_of in split:
        steps = jax.random.uniform(jax.random.fold_in(jax.random.fold_in(own_key, 6), axis_at), (shards_of,), jnp.float32, least / len(split), top_value / len(split))
        factor_of = factor_of * jnp.repeat(jnp.exp(steps), extent[axis_at] // shards_of).reshape((-1,) + (1,) * (len(extent) - 1 - axis_at))
    return factor_of


def length_profile(amount, total, bound, skew):
    portions = [(1 << 20) // math.isqrt(standing ** skew) + 1 for standing in range(2, amount + 1)]
    rest, holding = total - bound - (amount - 1), [1] * (amount - 1)
    while rest > 0:
        candidates = [i for i in range(amount - 1) if holding[i] < bound]
        whole, left = sum([portions[i] for i in candidates]), rest
        for i in candidates:
            extra = min(bound - holding[i], max(1, left * portions[i] // whole), rest)
            holding[i] = holding[i] + extra
            rest = rest - extra
    return np.array([bound] + holding)


def uneven_parts(key, count, total, bound, skew):
    if count == 2:
        one = jax.random.randint(key, (), max(1, total - bound), min(bound, total - 1) + 1)
        return jnp.stack([one, total - one])
    tallies = jnp.asarray(length_profile(count, total, bound, skew), jnp.int32)
    twos = (count - 1) // 2
    giver, taker = tallies[1:1 + 2 * twos:2], tallies[2:2 + 2 * twos:2]
    room = jnp.minimum(giver - 1, bound - taker)
    passed = jax.random.randint(jax.random.fold_in(key, 1), (twos,), 0, 1 << 20) % (room + 1)
    tallies = tallies.at[1:1 + 2 * twos:2].set(giver - passed).at[2:2 + 2 * twos:2].set(taker + passed)
    return tallies[jax.random.permutation(jax.random.fold_in(key, 2), count)]


def gaussian(stream_key, shape, scale, limit, shards=(), held_as=jnp.bfloat16):
    result = jax.random.normal(stream_key, shape, jnp.float32) * scale
    if len(shards) > 0:
        result = block_levels(stream_key, shape, shards, -0.22, 0.18) * result
    return jnp.clip(result, min=-limit, max=limit).astype(held_as)


def setup_inputs(seed: int = 0) -> dict:
    arg_keys = jax.random.split(jax.random.key(seed), 16)
    h_in = gaussian(arg_keys[0], (TOKENS, D), 1.0, 6.0, ((0, 32),), jnp.float32)
    w_z = gaussian(arg_keys[1], (LAYERS, D, INNER), D ** -0.5, 0.21875, ((1, 8), (2, 4)))
    w_x = gaussian(arg_keys[2], (LAYERS, D, INNER), D ** -0.5, 0.21875, ((1, 8), (2, 4)))
    w_bc = gaussian(arg_keys[3], (LAYERS, D, 2 * NSTATE), D ** -0.5, 0.21875, ((1, 32),))
    w_dt = gaussian(arg_keys[4], (LAYERS, D, HEADS), D ** -0.5, 0.21875, ((1, 8), (2, 4)))
    w_out = gaussian(arg_keys[5], (LAYERS, INNER, D), INNER ** -0.5, 0.15625, ((1, 4), (2, 8)))
    conv_x = jnp.clip(jax.random.uniform(arg_keys[6], (LAYERS, CONV + 1, INNER), jnp.float32, -0.5, 0.5) * block_levels(arg_keys[6], (LAYERS, CONV + 1, INNER), ((2, 4),), -0.4, 0.0), -0.5, 0.5)
    conv_bc = jnp.clip(jax.random.uniform(arg_keys[7], (LAYERS, CONV + 1, 2 * NSTATE), jnp.float32, -0.5, 0.5) * block_levels(arg_keys[7], (LAYERS, CONV + 1, 2 * NSTATE), ((2, 32),), -0.4, 0.0), -0.5, 0.5).astype(jnp.bfloat16)
    dt_bias = jnp.clip(-6.0 + 4.0 * jax.random.uniform(arg_keys[8], (LAYERS, HEADS), jnp.float32) ** block_levels(arg_keys[8], (LAYERS, HEADS), ((1, 4),), -0.2, 0.2), -6.0, -2.0)
    a_log = jnp.clip(2.8 * jax.random.uniform(arg_keys[9], (LAYERS, HEADS), jnp.float32) ** block_levels(arg_keys[9], (LAYERS, HEADS), ((1, 4),), -0.2, 0.2), 0.0, 2.8)
    d_skip = jnp.clip(0.5 + 1.0 * jax.random.uniform(arg_keys[10], (LAYERS, HEADS), jnp.float32) ** block_levels(arg_keys[10], (LAYERS, HEADS), ((1, 4),), -0.2, 0.2), 0.5, 1.5)
    rms_gain = jnp.clip(1.0 + 0.1 * jax.random.normal(arg_keys[11], (LAYERS, D), jnp.float32), 0.5, 1.5).astype(jnp.bfloat16)
    gnorm_gain = jnp.clip(1.0 + 0.1 * jax.random.normal(arg_keys[12], (LAYERS, INNER), jnp.float32), 0.5, 1.5)
    seg_ids = jax.vmap(lambda own: jnp.searchsorted(jnp.cumsum(uneven_parts(own, 8, SEQ, SEQ // 2, 2)), jnp.arange(SEQ), side="right"))(jax.random.split(arg_keys[13], SEQS)).reshape((SEQS, SEQ)).astype(jnp.int32)
    cotangent = gaussian(arg_keys[14], (TOKENS, D), 1.0, 6.0, ((0, 32),), jnp.float32)
    return dict(h_in=h_in, w_z=w_z, w_x=w_x, w_bc=w_bc, w_dt=w_dt, w_out=w_out, conv_x=conv_x, conv_bc=conv_bc, dt_bias=dt_bias, a_log=a_log, d_skip=d_skip, rms_gain=rms_gain, gnorm_gain=gnorm_gain, seg_ids=seg_ids, cotangent=cotangent)


EPS = 1e-05
HIGH = lax.Precision.HIGHEST

def product(left, right):
    return jnp.dot(left, right, preferred_element_type=jnp.float32)

def product_nt(left, right):
    return lax.dot_general(left, right, (((1,), (1,)), ((), ())), preferred_element_type=jnp.float32)

def product_tn(left, right):
    return lax.dot_general(left, right, (((0,), (0,)), ((), ())), preferred_element_type=jnp.float32)

def exact_nt(left, right):
    return lax.dot_general(left, right, (((1,), (1,)), ((), ())), precision=HIGH)

def exact_tn(left, right):
    return lax.dot_general(left, right, (((0,), (0,)), ((), ())), precision=HIGH)

def depthwise_conv(signal, weights, segment):
    width = weights.shape[0] - 1
    total = weights[width][None, :] + weights[width - 1][None, :] * signal
    for offset in range(1, width):
        earlier = jnp.concatenate([jnp.zeros((offset, signal.shape[1]), signal.dtype), signal[:-offset]], axis=0)
        earlier_seg = jnp.concatenate([jnp.full((offset,), -1, jnp.int32), segment[:-offset]])
        same_doc = (earlier_seg == segment)[:, None]
        total = total + weights[width - 1 - offset][None, :] * jnp.where(same_doc, earlier, 0.0)
    return jax.nn.silu(total)

def group_scan(inputs_x, decay, b_state, c_state, segment, block_len):
    length, heads, head_dim = inputs_x.shape
    state_cols = b_state.shape[1]
    blocks = length // block_len
    stacked = (inputs_x.reshape(blocks, block_len, heads, head_dim), decay.reshape(blocks, block_len, heads), b_state.reshape(blocks, block_len, state_cols), c_state.reshape(blocks, block_len, state_cols), segment.reshape(blocks, block_len))
    positions = jnp.arange(block_len)
    lower = positions[:, None] >= positions[None, :]

    def advance(carried, inputs_now):
        state, last_seg = carried
        block_x, block_decay, block_b, block_c, block_seg = inputs_now
        running = jnp.cumsum(block_decay, axis=0)
        masked = (lower & (block_seg[:, None] == block_seg[None, :]))[:, :, None]
        spread = running[:, None, :] - running[None, :, :]
        factors = jnp.where(masked, jnp.exp(jnp.where(masked, spread, 0.0)), 0.0)
        scores = jnp.dot(block_c, block_b.T, precision=HIGH)
        within = jnp.einsum('ijh,jhp->ihp', scores[:, :, None] * factors, block_x, precision=HIGH)
        carry_in = jnp.where((block_seg == last_seg)[:, None], jnp.exp(running), 0.0)
        from_state = jnp.einsum('in,hpn->ihp', block_c, state, precision=HIGH) * carry_in[:, :, None]
        end_seg = block_seg[block_len - 1]
        tail = jnp.where((block_seg == end_seg)[:, None], jnp.exp(running[block_len - 1][None, :] - running), 0.0)
        retain = jnp.where(end_seg == last_seg, jnp.exp(running[block_len - 1]), 0.0)
        new_state = state * retain[:, None, None] + jnp.einsum('jh,jhp,jn->hpn', tail, block_x, block_b, precision=HIGH)
        return ((new_state, end_seg), within + from_state)
    initial = (jnp.zeros((heads, head_dim, state_cols), inputs_x.dtype), jnp.array(-1, jnp.int32))
    _, outputs = lax.scan(advance, initial, stacked)
    return outputs.reshape(length, heads, head_dim)

def mixer_core(gate_pre, x_pre, bc_pre, step_pre, conv_inner, conv_shared, step_bias, log_rate, skip_gain, segment):
    heads = step_pre.shape[1]
    head_dim = x_pre.shape[1] // heads
    state_cols = bc_pre.shape[1] // 2
    x_act = depthwise_conv(x_pre, conv_inner, segment)
    bc_act = depthwise_conv(bc_pre, conv_shared, segment)
    step_size = jax.nn.softplus(step_pre + step_bias[None, :])
    decay = -step_size * jnp.exp(log_rate)[None, :]
    x_heads = x_act.reshape(x_act.shape[0], heads, head_dim)
    scanned = group_scan(x_heads * step_size[:, :, None], decay, bc_act[:, :state_cols], bc_act[:, state_cols:], segment, GROUP)
    mixed = scanned + skip_gain[None, :, None] * x_heads
    return mixed.reshape(x_pre.shape) * jax.nn.silu(gate_pre)

def sequence_pass(hidden, upstream, segment, params):
    w_z, w_x, w_bc, w_dt, w_out, conv_x, conv_bc, dt_bias, a_log, d_skip, rms_gain, gnorm_gain = params
    core = partial(mixer_core, segment=segment)
    saved = []
    for layer_index in range(LAYERS):
        scale = lax.rsqrt(lax.optimization_barrier(jnp.mean(hidden * hidden, axis=1, keepdims=True)) + EPS)
        normed = (hidden * scale * rms_gain[layer_index].astype(jnp.float32)[None, :]).astype(jnp.bfloat16)
        gate_pre = product(normed, w_z[layer_index])
        x_pre = product(normed, w_x[layer_index])
        bc_pre = product(normed, w_bc[layer_index])
        step_pre = product(normed, w_dt[layer_index])
        mixed = core(gate_pre, x_pre, bc_pre, step_pre, conv_x[layer_index], conv_bc[layer_index].astype(jnp.float32), dt_bias[layer_index], a_log[layer_index], d_skip[layer_index])
        gate_scale = lax.rsqrt(lax.optimization_barrier(jnp.mean(mixed * mixed, axis=1, keepdims=True)) + EPS)
        gated = (mixed * gate_scale * gnorm_gain[layer_index][None, :]).astype(jnp.bfloat16)
        saved.append((hidden, scale, normed, gate_pre, x_pre, bc_pre, step_pre, gate_scale, gated))
        hidden = hidden + product(gated, w_out[layer_index])
    results = [None] * LAYERS
    for layer_index in reversed(range(LAYERS)):
        hidden_in, scale, normed, gate_pre, x_pre, bc_pre, step_pre, gate_scale, gated = saved[layer_index]
        upstream_bf = upstream.astype(jnp.bfloat16)
        grad_out_w = product_tn(gated, upstream_bf)
        dgated = product_nt(upstream_bf, w_out[layer_index])
        mixed, pullback = jax.vjp(core, gate_pre, x_pre, bc_pre, step_pre, conv_x[layer_index], conv_bc[layer_index].astype(jnp.float32), dt_bias[layer_index], a_log[layer_index], d_skip[layer_index])
        normal_v = mixed * gate_scale
        grad_gnorm = lax.optimization_barrier(jnp.sum(dgated * normal_v, axis=0))
        dscaled = dgated * gnorm_gain[layer_index][None, :]
        dmixed = gate_scale * (dscaled - normal_v * lax.optimization_barrier(jnp.mean(dscaled * normal_v, axis=1, keepdims=True)))
        d_gate, d_units, d_bc, d_step, d_conv_x, d_conv_bc, d_bias, d_rate, d_skipgain = pullback(dmixed)
        gate_bf = d_gate.astype(jnp.bfloat16)
        units_bf = d_units.astype(jnp.bfloat16)
        step_bf = d_step.astype(jnp.bfloat16)
        d_normed = product_nt(gate_bf, w_z[layer_index]) + product_nt(units_bf, w_x[layer_index]) + product_nt(step_bf, w_dt[layer_index]) + exact_nt(d_bc, w_bc[layer_index].astype(jnp.float32))
        grad_wz = product_tn(normed, gate_bf)
        grad_wx = product_tn(normed, units_bf)
        grad_wdt = product_tn(normed, step_bf)
        grad_wbc = exact_tn(normed.astype(jnp.float32), d_bc)
        hnorm = hidden_in * scale
        grad_rms = lax.optimization_barrier(jnp.sum(d_normed * hnorm, axis=0))
        dhnorm = d_normed * rms_gain[layer_index].astype(jnp.float32)[None, :]
        upstream = upstream + scale * (dhnorm - hnorm * lax.optimization_barrier(jnp.mean(dhnorm * hnorm, axis=1, keepdims=True)))
        results[layer_index] = (grad_wz, grad_wx, grad_wbc, grad_wdt, grad_out_w, d_conv_x, d_conv_bc, d_bias, d_rate, d_skipgain, grad_rms, grad_gnorm)
    stacked = tuple((jnp.stack([results[index][member] for index in range(LAYERS)]) for member in range(12)))
    return (hidden, upstream, stacked)

def reference(h_in, w_z, w_x, w_bc, w_dt, w_out, conv_x, conv_bc, dt_bias, a_log, d_skip, rms_gain, gnorm_gain, seg_ids, cotangent):
    params = (w_z, w_x, w_bc, w_dt, w_out, conv_x, conv_bc, dt_bias, a_log, d_skip, rms_gain, gnorm_gain)
    seq_count = seg_ids.shape[0]
    hidden_all = h_in.reshape(seq_count, SEQ, D)
    cot_all = cotangent.reshape(seq_count, SEQ, D)
    totals = tuple((jnp.zeros(param.shape, jnp.float32) for param in params))

    def one_sequence(running, inputs_now):
        hidden, upstream, segment = inputs_now
        output, dinput, grads = sequence_pass(hidden, upstream, segment, params)
        return (tuple((first + second for first, second in zip(running, grads))), (output, dinput))
    totals, (outputs, dinputs) = lax.scan(one_sequence, totals, (hidden_all, cot_all, seg_ids))
    return (outputs.reshape(TOKENS, D), dinputs.reshape(TOKENS, D), totals[0], totals[1], totals[2], totals[3], totals[4], totals[5], totals[6], totals[7], totals[8], totals[9], totals[10], totals[11])
```

```python
from functools import partial

import jax
import jax.numpy as jnp
from jax import lax
from jax.experimental import pallas as pl
from jax.experimental.pallas import tpu as pltpu
from jax.sharding import PartitionSpec as P


GROUP = 128
LANES = 128
EPS = 1e-05
F32 = jnp.float32
BF16 = jnp.bfloat16
HIGH = lax.Precision.HIGHEST
INTERPRET = False


def mm(left, right):
    return jnp.dot(left, right, preferred_element_type=F32)


def mm_nt(left, right):
    return lax.dot_general(left, right, (((1,), (1,)), ((), ())), preferred_element_type=F32)


def mm_tn(left, right):
    return lax.dot_general(left, right, (((0,), (0,)), ((), ())), preferred_element_type=F32)


def high_low(value):
    high = value.astype(BF16)
    return high, (value - high.astype(F32)).astype(BF16)


def unit_map(heads, units):
    row = lax.broadcasted_iota(jnp.int32, (LANES, units), 0)
    col = lax.broadcasted_iota(jnp.int32, (LANES, units), 1)
    return jnp.where(row == col // (units // heads), 1.0, 0.0).astype(BF16)


def widen(per_head, umap):
    high, low = high_low(per_head)
    return mm(high, umap) + mm(low, umap)


def narrow(per_unit, umap):
    high, low = high_low(per_unit)
    return mm_nt(high, umap) + mm_nt(low, umap)


def sigmoid(value):
    return 1.0 / (1.0 + jnp.exp(-value))


def conv_sum(signal, taps, masks):
    total = taps[4:5] + taps[3:4] * signal
    for offset in range(1, 4):
        moved = pltpu.roll(signal, offset, 0)
        total = total + taps[3 - offset : 4 - offset] * (moved * masks[:, offset - 1 : offset])
    return total


def conv_back(d_act, pre, signal, taps, masks):
    rows = signal.shape[0]
    sg = sigmoid(pre)
    dc = d_act * (sg * (1.0 + pre * (1.0 - sg)))
    d_in = taps[3:4] * dc
    grads = {3: jnp.sum(dc * signal, axis=0, keepdims=True)}
    for offset in range(1, 4):
        masked = dc * masks[:, offset - 1 : offset]
        d_in = d_in + taps[3 - offset : 4 - offset] * pltpu.roll(masked, rows - offset, 0)
        grads[3 - offset] = jnp.sum(
            masked * pltpu.roll(signal, offset, 0), axis=0, keepdims=True
        )
    grads[4] = jnp.sum(dc, axis=0, keepdims=True)
    pad = jnp.zeros((3, signal.shape[1]), F32)
    return d_in, jnp.concatenate([grads[k] for k in range(5)] + [pad], axis=0)


def fill_rows(pieces, me, full):
    count = len(pieces)
    rows = pieces[0].shape[0]
    if count == 1:
        return pieces[0][...]
    for k, piece in enumerate(pieces):
        at = pl.multiple_of((me ^ k) * rows, rows)
        full[pl.ds(at, rows), :] = piece[...]
    return full[...]


def mixer_state(x_pre, bc_pre, stp, cx, cbc, hp, masks, heads):
    units = x_pre.shape[1]
    cols = bc_pre.shape[1] // 2
    rows = x_pre.shape[0]
    blocks = rows // GROUP
    umap = unit_map(heads, units)
    c_x = conv_sum(x_pre, cx, masks)
    c_bc = conv_sum(bc_pre, cbc, masks)
    x_act = c_x * sigmoid(c_x)
    bc_act = c_bc * sigmoid(c_bc)
    raw = stp + hp[0:1]
    step = jnp.maximum(raw, 0.0) + jnp.log1p(jnp.exp(-jnp.abs(raw)))
    rate = -step * jnp.exp(hp[1:2])
    pos_r = lax.broadcasted_iota(jnp.int32, (GROUP, GROUP), 0)
    pos_c = lax.broadcasted_iota(jnp.int32, (GROUP, GROUP), 1)
    lower = pos_r >= pos_c
    tri = jnp.where(lower, 1.0, 0.0)
    run = [
        jnp.dot(tri, rate[i * GROUP : (i + 1) * GROUP], precision=HIGH, preferred_element_type=F32)
        for i in range(blocks)
    ]
    u = [jnp.exp(r) for r in run]
    v = [jnp.exp(r[GROUP - 1 : GROUP] - r) for r in run]
    wide = widen(jnp.concatenate([step] + u + v + [jnp.broadcast_to(hp[2:3], (8, LANES))], axis=0), umap)
    step_u = wide[:rows]
    u_u = wide[rows : 2 * rows]
    v_u = wide[2 * rows : 3 * rows]
    skip_u = wide[3 * rows : 3 * rows + 1]
    b_bf = bc_act[:, :cols].astype(BF16)
    c_bf = bc_act[:, cols:].astype(BF16)
    xs = x_act * step_u
    return dict(
        umap=umap, c_x=c_x, c_bc=c_bc, x_act=x_act, raw=raw, step=step, rate=rate, lower=lower,
        tri=tri, run=run, step_u=step_u, u_u=u_u, v_u=v_u, skip_u=skip_u, b=b_bf, c=c_bf, xs=xs,
        blocks=blocks, heads=heads, units=units,
    )


def block_of(value, i):
    return value[i * GROUP : (i + 1) * GROUP]


def pair_lanes(heads, units):
    per = units // heads
    return LANES // per, per


def decay_tile(st, i, h, run_t):
    spread = st["run"][i][:, h : h + 1] - run_t[h : h + 1, :]
    return jnp.exp(jnp.where(st["keep"][i], spread, -1e30))


def scores_of(st, segc, segr, i):
    raw = mm_nt(block_of(st["c"], i), st["b"][: (i + 1) * GROUP])
    same = block_of(segc, i) == segr[:, : (i + 1) * GROUP]
    keep = same[:, i * GROUP :] & st["lower"]
    off = None
    if i:
        off = jnp.where(same[:, : i * GROUP], raw[:, : i * GROUP], 0.0)
    return off, raw[:, i * GROUP :], keep, same


def mixer_fwd_kernel(heads, count, *refs):
    me, nrm, wbc, wdt, cx, cbc, hp, segm, segr = refs[:9]
    pieces = refs[9 : 9 + count]
    x_ref, bc_ref, st_ref, y_ref = refs[9 + count : 13 + count]
    full = refs[13 + count]
    wx = fill_rows(pieces, me[0], full)
    normed = nrm[...]
    x_pre = mm(normed, wx)
    bc_pre = mm(normed, wbc[...])
    stp = mm(normed, wdt[...])
    x_ref[...] = x_pre
    bc_ref[...] = bc_pre
    st_ref[...] = stp
    masks = segm[...]
    segc, segl = masks[:, 3:4], segr[...]
    st = mixer_state(x_pre, bc_pre, stp, cx[...], cbc[...], hp[...], masks, heads)
    st["keep"] = {}
    units = st["units"]
    group, per = pair_lanes(heads, units)
    lane = lax.broadcasted_iota(jnp.int32, (GROUP, LANES), 1)
    xs_bf = st["xs"].astype(BF16)
    carried = []
    for i in range(st["blocks"]):
        off, diag, keep, _ = scores_of(st, segc, segl, i)
        st["keep"][i] = keep
        run_t = st["run"][i].T
        parts = []
        for p in range(units // LANES):
            x_pair = block_of(xs_bf, i)[:, p * LANES : (p + 1) * LANES]
            total = None
            for g in range(group):
                tile = (diag * decay_tile(st, i, p * group + g, run_t)).astype(BF16)
                part = mm(tile, x_pair)
                total = part if total is None else jnp.where(lane >= g * per, part, total)
            parts.append(total)
        y = jnp.concatenate(parts, axis=1) + st["skip_u"] * block_of(st["x_act"], i)
        u_i = block_of(st["u_u"], i)
        if i:
            held = jnp.concatenate([c.astype(BF16) for c in carried], axis=0)
            y = y + u_i * mm(off.astype(BF16), held)
        y_ref[i * GROUP : (i + 1) * GROUP, :] = y
        end = u_i[GROUP - 1 : GROUP]
        carried = [c * end for c in carried]
        carried.append(block_of(st["xs"], i) * block_of(st["v_u"], i))


def gate_fwd_kernel(last, count, mp_count, *refs):
    me, nrm, y, gg = refs[:4]
    at = 4
    wz_p = refs[at : at + count]
    at += count
    wo_p = refs[at : at + count]
    at += count
    if last:
        cot_p = refs[at : at + mp_count]
        at += mp_count
    gate_ref = refs[at]
    outs = refs[at + 1 : at + 1 + mp_count]
    at += 1 + mp_count
    if last:
        stat_ref, dg_ref, up_ref = refs[at : at + 3]
        at += 3
    wz_s, wo_s, po_s = refs[at : at + 3]
    wz = fill_rows(wz_p, me[0], wz_s)
    wo = fill_rows(wo_p, me[0], wo_s)
    gate = mm(nrm[...], wz)
    gate_ref[...] = gate
    mixed = y[...] * (gate * sigmoid(gate))
    weighted = mixed * gg[...]
    squares = jnp.sum(mixed * mixed, axis=1, keepdims=True)
    width = wo.shape[0]
    po_s[:, :width] = mm_nt(weighted.astype(BF16), wo).astype(BF16)
    high, low = high_low(squares)
    rows = squares.shape[0]
    lane = lax.broadcasted_iota(jnp.int32, (rows, LANES), 1)
    extra = jnp.where(lane == 0, high.astype(F32), jnp.where(lane == 1, low.astype(F32), 0.0))
    po_s[:, width:] = extra.astype(BF16)
    own = rows // mp_count
    for q in range(mp_count):
        begin = pl.multiple_of((me[1] ^ q) * own, own)
        outs[q][...] = po_s[pl.ds(begin, own), :]
    if last:
        ups = fill_rows(cot_p, me[1], up_ref)
        if mp_count == 1:
            up_ref[...] = ups
        dg = mm(ups, wo)
        dg_ref[...] = dg
        cross = jnp.sum(dg * weighted, axis=1, keepdims=True)
        stat = jnp.where(lane == 0, squares, jnp.where(lane == 1, cross, 0.0))
        stat_ref[...] = stat.T[:8, :]


def gate_bwd_kernel(last, count, mp_count, inner, *refs):
    me, nrm, y, gate, gg = refs[:5]
    at = 5
    if last:
        stats, dg_in, ups_ref = refs[at : at + 3]
        at += 3
    else:
        ups_p = refs[at : at + mp_count]
        at += mp_count
        wo_p = refs[at : at + count]
        at += count
    dy_ref, dgate_ref, ggn_ref = refs[at : at + 3]
    outs = refs[at + 3 : at + 3 + count]
    at += 3 + count
    scratch = refs[at:]
    rows = y.shape[0]
    width = nrm.shape[1]
    if last:
        total = stats[0]
        for k in range(1, stats.shape[0]):
            total = total + stats[k]
        pad = jnp.zeros((LANES - 8, rows), F32)
        cols = jnp.concatenate([total, pad], axis=0).T
        scale = lax.rsqrt(cols[:, 0:1] / inner + EPS)
        kappa = scale * scale * scale * cols[:, 1:2] / inner
        dg = dg_in[...]
        ups = ups_ref[...]
    else:
        ext = fill_rows(ups_p, me[1], scratch[1])
        tail = ext[:, width:].astype(F32)
        scale = tail[:, 0:1] + tail[:, 1:2]
        kappa = tail[:, 2:3] + tail[:, 3:4]
        ups = ext[:, :width]
        wo = fill_rows(wo_p, me[0], scratch[2])
        dg = mm(ups, wo)
    g = gate[...]
    sg = sigmoid(g)
    silu = g * sg
    mixed = y[...] * silu
    scaled = dg * scale
    ggn = jnp.sum(scaled * mixed, axis=0, keepdims=True)
    ggn_ref[...] = jnp.concatenate([ggn, jnp.zeros((7, ggn.shape[1]), F32)], axis=0)
    d_mixed = scaled * gg[...] - mixed * kappa
    d_gate = (d_mixed * y[...] * (sg * (1.0 + g * (1.0 - sg)))).astype(BF16)
    dgate_ref[...] = d_gate
    dy_ref[...] = d_mixed * silu
    gated = (mixed * scale * gg[...]).astype(BF16)
    grads = scratch[0]
    grads[:width, :] = mm_tn(nrm[...], d_gate).astype(BF16)
    grads[width:, :] = mm_tn(ups, gated).astype(BF16)
    own = width // count
    for k in range(count):
        begin = pl.multiple_of((me[0] ^ k) * own, own)
        outs[k][:own, :] = grads[pl.ds(begin, own), :]
        outs[k][own:, :] = grads[pl.ds(pl.multiple_of(width + begin, own), own), :]


def mixer_bwd_kernel(heads, count, mp_count, shared, *refs):
    me, nrm, xp, bp, sp, dy_in, dgate, wbc, wdt, cx, cbc, hp, segm, segr, gain, ggn = refs[:16]
    at = 16
    wz_p = refs[at : at + count]
    at += count
    wx_p = refs[at : at + count]
    at += count
    dn_outs = refs[at : at + mp_count]
    at += mp_count
    sm_outs = refs[at : at + (mp_count if shared else 2)]
    at += mp_count if shared else 2
    gx_outs = refs[at : at + count]
    at += count
    wz_s, wx_s, dn_s, gx_s, gw_s, gc_s, sm_s = refs[at : at + 7]
    x_pre, bc_pre, stp = xp[...], bp[...], sp[...]
    masks = segm[...]
    segc, segl = masks[:, 3:4], segr[...]
    st = mixer_state(x_pre, bc_pre, stp, cx[...], cbc[...], hp[...], masks, heads)
    st["keep"] = {}
    units, blocks, umap = st["units"], st["blocks"], st["umap"]
    group, per = pair_lanes(heads, units)
    lane = lax.broadcasted_iota(jnp.int32, (GROUP, LANES), 1)
    pos_r = lax.broadcasted_iota(jnp.int32, (GROUP, GROUP), 0)
    pos_c = lax.broadcasted_iota(jnp.int32, (GROUP, GROUP), 1)
    strict = pos_r > pos_c
    upper = jnp.where(pos_c >= pos_r, 1.0, 0.0)
    before = jnp.where(strict, 1.0, 0.0)
    dy = dy_in[...]
    xs_bf = st["xs"].astype(BF16)
    dy_bf = dy.astype(BF16)
    dyu = dy * st["u_u"]
    dyu_bf = dyu.astype(BF16)
    held = [[]]
    for i in range(blocks):
        end = block_of(st["u_u"], i)[GROUP - 1 : GROUP]
        new = [c * end for c in held[i]]
        new.append(block_of(st["xs"], i) * block_of(st["v_u"], i))
        held.append(new)
    later = None
    d_b = [None] * blocks
    d_c = [None] * blocks
    d_xs = [None] * blocks
    d_rate = [None] * blocks
    for i in reversed(range(blocks)):
        off, diag, keep, same = scores_of(st, segc, segl, i)
        st["keep"][i] = keep
        run_t = st["run"][i].T
        d_diag = None
        d_run = None
        parts = []
        for p in range(units // LANES):
            x_pair = block_of(xs_bf, i)[:, p * LANES : (p + 1) * LANES]
            dy_pair = block_of(dy_bf, i)[:, p * LANES : (p + 1) * LANES]
            total = None
            for g in range(group):
                h = p * group + g
                decay = decay_tile(st, i, h, run_t)
                tile = diag * decay
                mine = (lane >= g * per) & (lane < (g + 1) * per)
                d_tile = mm_nt(jnp.where(mine, dy_pair, jnp.zeros_like(dy_pair)), x_pair)
                part = mm_tn(tile.astype(BF16), dy_pair)
                total = part if total is None else jnp.where(lane >= g * per, part, total)
                term = d_tile * decay
                d_diag = term if d_diag is None else d_diag + term
                flow = jnp.where(strict, d_tile * tile, 0.0)
                high, low = high_low(flow)
                pick = jnp.where(pos_c == h, 1.0, 0.0).astype(BF16)
                turn = (mm(high, pick) + mm(low, pick)) - (mm_tn(high, pick) + mm_tn(low, pick))
                d_run = turn if d_run is None else d_run + turn
            parts.append(total)
        grad_xs = jnp.concatenate(parts, axis=1)
        d_scores = d_diag
        direct = None
        if i:
            rows_bf = block_of(dyu_bf, i)
            z_bf = jnp.concatenate([c.astype(BF16) for c in held[i]], axis=0)
            off_bf = off.astype(BF16)
            d_run = d_run + narrow(block_of(dyu, i) * mm(off_bf, z_bf), umap)
            d_off = jnp.where(same[:, : i * GROUP], mm_nt(rows_bf, z_bf), 0.0)
            d_scores = jnp.concatenate([d_off, d_diag], axis=1)
            direct = mm_tn(off_bf, rows_bf)
        rate_grad = jnp.dot(upper, d_run, precision=HIGH, preferred_element_type=F32)
        end = block_of(st["u_u"], i)[GROUP - 1 : GROUP]
        if later is not None:
            into = later[i]
            grad_xs = grad_xs + into * block_of(st["v_u"], i)
            q = narrow(into * held[i + 1][i], umap)
            rate_grad = rate_grad + jnp.dot(before, q, precision=HIGH, preferred_element_type=F32)
            if i:
                through = None
                for j in range(i):
                    part = jnp.sum(later[j] * held[i][j], axis=0, keepdims=True)
                    through = part if through is None else through + part
                through = jnp.broadcast_to(through * end, (8, units))
                rate_grad = rate_grad + narrow(through, umap)[0:1]
        new = []
        for j in range(i):
            term = direct[j * GROUP : (j + 1) * GROUP]
            if later is not None:
                term = term + later[j] * end
            new.append(term)
        later = new
        d_xs[i] = grad_xs
        d_rate[i] = rate_grad
        ds_bf = d_scores.astype(BF16)
        d_c[i] = mm(ds_bf, st["b"][: (i + 1) * GROUP])
        back = mm_tn(ds_bf, block_of(st["c"], i))
        for j in range(i + 1):
            term = back[j * GROUP : (j + 1) * GROUP]
            d_b[j] = term if d_b[j] is None else d_b[j] + term
    d_xs = jnp.concatenate(d_xs, axis=0)
    d_rate = jnp.concatenate(d_rate, axis=0)
    d_bc_act = jnp.concatenate(
        [jnp.concatenate(d_b, axis=0), jnp.concatenate(d_c, axis=0)], axis=1
    )
    d_x_act = d_xs * st["step_u"] + dy * st["skip_u"]
    d_step = narrow(d_xs * st["x_act"], umap) - d_rate * jnp.exp(hp[1:2, :])
    skip_row = jnp.broadcast_to(jnp.sum(dy * st["x_act"], axis=0, keepdims=True), (8, units))
    g_skip = narrow(skip_row, umap)[0:1]
    g_rate = jnp.sum(d_rate * st["rate"], axis=0, keepdims=True)
    d_stp = d_step * sigmoid(st["raw"])
    g_bias = jnp.sum(d_stp, axis=0, keepdims=True)
    head = lax.broadcasted_iota(jnp.int32, d_stp.shape, 1)
    d_stp_bf = jnp.where(head < heads, d_stp, 0.0).astype(BF16)
    d_x, g_cx = conv_back(d_x_act, st["c_x"], x_pre, cx[...], masks)
    d_bc, g_cbc = conv_back(d_bc_act, st["c_bc"], bc_pre, cbc[...], masks)
    d_x_bf = d_x.astype(BF16)
    d_bc_bf = d_bc.astype(BF16)
    wz = fill_rows(wz_p, me[0], wz_s)
    wx = fill_rows(wx_p, me[0], wx_s)
    dn = mm_nt(dgate[...], wz) + mm_nt(d_x_bf, wx)
    dn = dn + mm_nt(d_stp_bf, wdt[...]) + mm_nt(d_bc_bf, wbc[...])
    normed = nrm[...]
    hnorm = normed.astype(F32) / gain[...]
    g_gain = jnp.sum(dn * hnorm, axis=0, keepdims=True)
    width = normed.shape[1]
    rows = normed.shape[0]
    dn_s[...] = dn.astype(BF16)
    own = rows // mp_count
    for q in range(mp_count):
        begin = pl.multiple_of((me[1] ^ q) * own, own)
        dn_outs[q][...] = dn_s[pl.ds(begin, own), :]
    bc_units = d_bc.shape[1]
    gw_s[:, :bc_units] = mm_tn(normed, d_bc_bf)
    g_high = g_gain.astype(BF16).astype(F32)
    gain_rows = jnp.concatenate([g_high, g_gain - g_high, jnp.zeros((LANES - 2, width), F32)], axis=0)
    gw_s[:, bc_units:] = gain_rows.T
    c_high = g_cbc.astype(BF16).astype(F32)
    conv_rows = jnp.concatenate([c_high, g_cbc - c_high, jnp.zeros((LANES - 16, bc_units), F32)], axis=0)
    gc_s[...] = conv_rows.T
    if shared:
        w_own = width // (shared * mp_count)
        c_own = bc_units // (shared * mp_count)
        for q in range(mp_count):
            for k in range(shared):
                slot = k * mp_count + (me[1] ^ q)
                sm_s[k * w_own : (k + 1) * w_own, :] = gw_s[
                    pl.ds(pl.multiple_of(slot * w_own, w_own), w_own), :
                ]
                base = shared * w_own + k * c_own
                sm_s[base : base + c_own, :LANES] = gc_s[
                    pl.ds(pl.multiple_of(slot * c_own, c_own), c_own), :
                ]
                sm_s[base : base + c_own, LANES:] = jnp.zeros((c_own, bc_units), F32)
            sm_outs[q][...] = sm_s[...].astype(BF16)
    else:
        sm_outs[0][...] = gw_s[...]
        sm_outs[1][...] = gc_s[...]
    gx_s[...] = mm_tn(normed, d_x_bf).astype(BF16)
    heads_row = jnp.concatenate([g_bias, g_rate, g_skip], axis=1)
    if heads_row.shape[1] < units:
        heads_row = jnp.concatenate(
            [heads_row, jnp.zeros((1, units - heads_row.shape[1]), F32)], axis=1
        )
    small = jnp.concatenate([g_cx[:5], ggn[0:1, :], heads_row, jnp.zeros((1, units), F32)], axis=0)
    s_high, s_low = high_low(small)
    g_dt = mm_tn(d_stp_bf, normed)[:8]
    halves = [g_dt[:, k * units : (k + 1) * units] for k in range(width // units)]
    tail = jnp.concatenate([s_high.astype(F32), s_low.astype(F32)] + halves, axis=0).astype(BF16)
    own = width // count
    for k in range(count):
        begin = pl.multiple_of((me[0] ^ k) * own, own)
        gx_outs[k][:own, :] = gx_s[pl.ds(begin, own), :]
        gx_outs[k][own:, :] = tail


def after_fwd_kernel(last, mp_count, inner, *refs):
    parts = refs[:mp_count]
    hidden, gain = refs[mp_count : mp_count + 2]
    outs = refs[mp_count + 2 :]
    total = parts[0][...].astype(F32)
    for part in parts[1:]:
        total = total + part[...].astype(F32)
    width = hidden.shape[1]
    squares = total[:, width : width + 1] + total[:, width + 1 : width + 2]
    scale = lax.rsqrt(squares / inner + EPS)
    branch = total[:, :width] * scale
    new = hidden[...] + branch
    outs[0][...] = new
    if not last:
        norm = lax.rsqrt(jnp.mean(new * new, axis=1, keepdims=True) + EPS)
        outs[1][...] = (new * norm * gain[...]).astype(BF16)
        outs[2][...] = branch
        outs[3][...] = scale


def after_bwd_kernel(first, mp_count, count, shared, inner, *refs):
    me = refs[0]
    parts = refs[1 : 1 + mp_count]
    at = 1 + mp_count
    sm_parts = ()
    if shared:
        sm_parts = refs[at : at + mp_count]
        at += mp_count
    ups, hidden, gain = refs[at : at + 3]
    at += 3
    if not first:
        branch, gscale = refs[at : at + 2]
        at += 2
    up_ref = refs[at]
    at += 1
    if not first:
        ext_ref = refs[at]
        at += 1
    dn = parts[0][...].astype(F32)
    for part in parts[1:]:
        dn = dn + part[...].astype(F32)
    h = hidden[...]
    scale = lax.rsqrt(jnp.mean(h * h, axis=1, keepdims=True) + EPS)
    hnorm = h * scale
    dh = dn * gain[...]
    new = ups[...] + scale * (dh - hnorm * jnp.mean(dh * hnorm, axis=1, keepdims=True))
    up_ref[...] = new
    if not first:
        rounded = new.astype(BF16)
        width = h.shape[1]
        gs = gscale[...]
        dot = jnp.sum(rounded.astype(F32) * branch[...], axis=1, keepdims=True)
        kappa = gs * gs * dot / inner
        lane = lax.broadcasted_iota(jnp.int32, (h.shape[0], LANES), 1)
        s_high, s_low = high_low(gs)
        k_high, k_low = high_low(kappa)
        extra = jnp.zeros((h.shape[0], LANES), F32)
        for at_lane, col in enumerate((s_high, s_low, k_high, k_low)):
            extra = jnp.where(lane == at_lane, col.astype(F32), extra)
        ext_ref[:, :width] = rounded
        ext_ref[:, width:] = extra.astype(BF16)
    if shared:
        sm_outs = refs[at : at + count]
        total_s, mix_s = refs[at + count : at + count + 2]
        total = sm_parts[0][...].astype(F32)
        for part in sm_parts[1:]:
            total = total + part[...].astype(F32)
        bc_units = total.shape[1] - LANES
        w_rows = gain.shape[1] // mp_count
        w_own = w_rows // count
        c_own = (total.shape[0] - w_rows) // count
        tail = total[:w_rows, bc_units:]
        lane = lax.broadcasted_iota(jnp.int32, tail.shape, 1)
        joined = tail[:, 0:1] + tail[:, 1:2]
        j_high = joined.astype(BF16).astype(F32)
        total_s[:w_rows, :bc_units] = total[:w_rows, :bc_units]
        total_s[:w_rows, bc_units:] = jnp.where(
            lane == 0, j_high, jnp.where(lane == 1, joined - j_high, 0.0)
        )
        conv = total[w_rows:, :LANES]
        lane = lax.broadcasted_iota(jnp.int32, conv.shape, 1)
        joined = jnp.where(lane < 8, conv + pltpu.roll(conv, LANES - 8, 1), 0.0)
        j_high = joined.astype(BF16).astype(F32)
        total_s[w_rows:, :LANES] = j_high + pltpu.roll(joined - j_high, 8, 1)
        total_s[w_rows:, LANES:] = jnp.zeros((total.shape[0] - w_rows, bc_units), F32)
        for k in range(count):
            slot = me[0] ^ k
            mix_s[:w_own, :] = total_s[pl.ds(pl.multiple_of(slot * w_own, w_own), w_own), :]
            mix_s[w_own:, :] = total_s[
                pl.ds(pl.multiple_of(w_rows + slot * c_own, c_own), c_own), :
            ]
            sm_outs[k][...] = mix_s[...].astype(BF16)


def call(kernel, name, inputs, outputs, scratch=(), flops=1 << 28):
    specs = []
    for value in inputs:
        space = pltpu.SMEM if value.dtype == jnp.int32 and value.ndim == 1 else pltpu.VMEM
        specs.append(pl.BlockSpec(memory_space=space))
    size = sum(v.size * v.dtype.itemsize for v in inputs)
    size += sum(v.size * v.dtype.itemsize for v in outputs)
    return pl.pallas_call(
        kernel,
        out_shape=[jax.ShapeDtypeStruct(o.shape, o.dtype) for o in outputs],
        in_specs=specs,
        out_specs=[pl.BlockSpec(memory_space=pltpu.VMEM) for _ in outputs],
        scratch_shapes=list(scratch),
        cost_estimate=pl.CostEstimate(flops=flops, bytes_accessed=size, transcendentals=0),
        compiler_params=pltpu.CompilerParams(vmem_limit_bytes=60 << 20),
        interpret=INTERPRET,
        name=name,
    )(*inputs)


def shape(dims, dtype):
    return jax.ShapeDtypeStruct(tuple(dims), dtype)


def partners(axis, k):
    return [(i, i ^ k) for i in range(lax.axis_size(axis))]


def spread(value, axis):
    n = lax.axis_size(axis)
    return [value] + [lax.ppermute(value, axis, partners(axis, k)) for k in range(1, n)]


def exchange(values, axis):
    n = lax.axis_size(axis)
    return [values[0]] + [lax.ppermute(values[k], axis, partners(axis, k)) for k in range(1, n)]


def in_order(pieces, me):
    stack = jnp.stack(pieces)
    n = stack.shape[0]
    bit = 1
    while bit < n:
        halves = stack.reshape((n // (2 * bit), 2, bit) + stack.shape[1:])
        swapped = jnp.where((me & bit) != 0, halves[:, ::-1], halves)
        stack = swapped.reshape(stack.shape)
        bit *= 2
    return stack


def add_up(pieces):
    total = pieces[0].astype(F32)
    for piece in pieces[1:]:
        total = total + piece.astype(F32)
    return total


def body(
    h_in,
    w_z,
    w_x,
    w_bc,
    w_dt,
    w_out,
    conv_x,
    conv_bc,
    dt_bias,
    a_log,
    d_skip,
    rms_gain,
    gnorm_gain,
    seg_ids,
    cotangent,
):
    dp, mp = lax.axis_size("dp"), lax.axis_size("mp")
    direct = dp <= 8 and dp & (dp - 1) == 0
    layers, width_own, units = w_z.shape
    width = h_in.shape[1]
    tokens = h_in.shape[0] * mp
    own = h_in.shape[0]
    heads = w_dt.shape[2]
    bc_units = w_bc.shape[2]
    taps = conv_x.shape[1]
    inner = units * mp
    my_dp, my_mp = lax.axis_index("dp"), lax.axis_index("mp")
    me = jnp.stack([my_dp if direct else jnp.zeros_like(my_dp), my_mp]).astype(jnp.int32)
    count = dp if direct else 1
    w_rows = width // count

    def fetch(value):
        if direct:
            return spread(value, "dp")
        return [lax.all_gather(value, "dp", axis=0, tiled=True)]

    out_t = jnp.swapaxes(w_out, 1, 2)
    if direct:
        own_w = w_bc.shape[1]
        own_c = conv_bc.shape[2]
        split = width_own // own_w
        dt_cols = jnp.pad(
            w_dt.reshape(layers, split, own_w, heads), ((0, 0), (0, 0), (0, 0), (0, 8 - heads % 8 if heads % 8 else 0))
        )
        dt_cols = jnp.swapaxes(dt_cols, 1, 2).reshape(layers, own_w, -1)
        top = jnp.concatenate(
            [w_bc, jnp.pad(rms_gain[:, :, None], ((0, 0), (0, 0), (0, 7))), dt_cols], axis=2
        )
        wide_sm = bc_units + LANES
        top = jnp.pad(top, ((0, 0), (0, 0), (0, wide_sm - top.shape[2])))
        low = jnp.pad(jnp.swapaxes(conv_bc, 1, 2), ((0, 0), (0, 0), (0, wide_sm - taps)))
        packed = jnp.concatenate([top, low], axis=1)
        got = in_order(spread(packed.reshape(-1, wide_sm), "dp"), my_dp)
        wx_p = [fetch(w_x[0])]
        every = in_order(spread(got.reshape(-1, wide_sm), "mp"), my_mp)
        every = every.reshape(mp, dp, layers, own_w + own_c, wide_sm)
        every = jnp.transpose(every, (2, 1, 0, 3, 4))
        wbc = every[:, :, :, :own_w, :bc_units].reshape(layers, width, bc_units)
        gains = every[:, :, :, :own_w, bc_units].reshape(layers, width)
        cbc = every[:, :, :, own_w:, :taps].reshape(layers, bc_units, taps)
        cbc = jnp.swapaxes(cbc, 1, 2).astype(F32)
        mine = got.reshape(dp, layers, own_w + own_c, wide_sm)[:, :, :own_w]
        h_pad = (heads + 7) // 8 * 8
        mine = mine[..., bc_units + 8 : bc_units + 8 + split * h_pad]
        mine = mine.reshape(dp, layers, own_w, split, h_pad)
        wdt = jnp.transpose(mine, (1, 0, 3, 2, 4)).reshape(layers, width, h_pad)
        wdt = jnp.pad(wdt, ((0, 0), (0, 0), (0, LANES - h_pad)))
    else:
        both = ("dp", "mp")
        wbc = lax.all_gather(w_bc, both, axis=1, tiled=True)
        gains = lax.all_gather(rms_gain, both, axis=1, tiled=True)
        cbc = lax.all_gather(conv_bc, both, axis=2, tiled=True).astype(F32)
        wdt = lax.all_gather(w_dt, "dp", axis=1, tiled=True)
        wdt = jnp.pad(wdt, ((0, 0), (0, 0), (0, LANES - heads)))
        wx_p = [fetch(w_x[0])]
    cbc = jnp.pad(cbc, ((0, 0), (0, 8 - taps), (0, 0)))
    gains = gains.astype(F32)
    wz_p = [fetch(w_z[0])]
    wo_p = [fetch(out_t[0])]
    for layer in range(1, layers):
        wx_p.append(fetch(w_x[layer]))
        wz_p.append(fetch(w_z[layer]))
        wo_p.append(fetch(out_t[layer]))

    segment = seg_ids[0]
    seg_f = segment.astype(F32)
    cols = []
    for offset in range(1, 4):
        earlier = jnp.concatenate([jnp.full((offset,), -1, jnp.int32), segment[:-offset]])
        cols.append((earlier == segment).astype(F32))
    segm = jnp.stack(cols + [seg_f], axis=1)
    segr = seg_f[None, :]
    hp = jnp.stack([dt_bias, a_log, d_skip], axis=1)
    hp = jnp.pad(hp, ((0, 0), (0, 5), (0, LANES - heads)))
    cx = jnp.pad(conv_x, ((0, 0), (0, 8 - taps), (0, 0)))

    scale = lax.rsqrt(jnp.mean(h_in * h_in, axis=1, keepdims=True) + EPS)
    normed = lax.all_gather((h_in * scale).astype(BF16), "mp", axis=0, tiled=True)
    normed = (normed.astype(F32) * gains[0][None, :]).astype(BF16)
    cot_p = spread(cotangent.astype(BF16), "mp")

    hidden = h_in
    saved = []
    for layer in range(layers):
        last = layer == layers - 1
        with jax.named_scope(f"fwd_{layer}"):
            x_pre, bc_pre, stp, y = call(
                partial(mixer_fwd_kernel, heads, count),
                "mixer_fwd",
                [me, normed, wbc[layer], wdt[layer], cx[layer], cbc[layer], hp[layer], segm, segr]
                + wx_p[layer],
                [
                    shape((tokens, units), F32),
                    shape((tokens, bc_units), F32),
                    shape((tokens, LANES), F32),
                    shape((tokens, units), F32),
                ],
                [pltpu.VMEM((width, units), BF16)],
                flops=8 << 30,
            )
            gg = gnorm_gain[layer][None, :]
            outs = [shape((tokens, units), F32)]
            outs += [shape((own, width + LANES), BF16)] * mp
            ins = [me, normed, y, gg] + wz_p[layer] + wo_p[layer]
            if last:
                ins += cot_p
                outs += [
                    shape((8, tokens), F32),
                    shape((tokens, units), F32),
                    shape((tokens, width), BF16),
                ]
            res = call(
                partial(gate_fwd_kernel, last, count, mp),
                "gate_fwd",
                ins,
                outs,
                [
                    pltpu.VMEM((width, units), BF16),
                    pltpu.VMEM((width, units), BF16),
                    pltpu.VMEM((tokens, width + LANES), BF16),
                ],
                flops=4 << 30,
            )
            gate, parts = res[0], res[1 : 1 + mp]
            if last:
                stats = lax.all_gather(res[1 + mp], "mp", axis=0)
                dg, ups_bf = res[2 + mp], res[3 + mp]
            got = exchange(parts, "mp")
            keep = dict(hidden=hidden, normed=normed, x_pre=x_pre, bc_pre=bc_pre, stp=stp, y=y, gate=gate, gg=gg)
            nxt = gains[min(layer + 1, layers - 1)][None, :]
            outs = [shape((own, width), F32)]
            if not last:
                outs += [
                    shape((own, width), BF16),
                    shape((own, width), F32),
                    shape((own, 1), F32),
                ]
            res = call(
                partial(after_fwd_kernel, last, mp, float(inner)),
                "after_fwd",
                got + [hidden, nxt],
                outs,
                flops=1 << 28,
            )
            hidden = res[0]
            if not last:
                keep["branch"], keep["gscale"] = res[2], res[3]
                normed = lax.all_gather(res[1], "mp", axis=0, tiled=True)
            saved.append(keep)

    upstream = cotangent
    results = [None] * layers
    ext_p = None
    for layer in reversed(range(layers)):
        last = layer == layers - 1
        keep = saved[layer]
        with jax.named_scope(f"bwd_{layer}"):
            ins = [me, keep["normed"], keep["y"], keep["gate"], keep["gg"]]
            scratch = [pltpu.VMEM((2 * width, units), BF16)]
            if last:
                ins += [stats, dg, ups_bf]
            else:
                ins += ext_p + wo_p[layer]
                scratch += [
                    pltpu.VMEM((tokens, width + LANES), BF16),
                    pltpu.VMEM((width, units), BF16),
                ]
            res = call(
                partial(gate_bwd_kernel, last, count, mp, float(inner)),
                "gate_bwd",
                ins,
                [
                    shape((tokens, units), F32),
                    shape((tokens, units), BF16),
                    shape((8, units), F32),
                ]
                + [shape((2 * w_rows, units), BF16)] * count,
                scratch,
                flops=6 << 30,
            )
            dy, dgate, ggn = res[:3]
            zo_grads = res[3:]
            shared = dp if direct else 0
            sm_rows = (width + bc_units) // mp
            outs = [shape((own, width), BF16)] * mp
            if shared:
                outs += [shape((sm_rows, bc_units + LANES), BF16)] * mp
            else:
                outs += [shape((width, bc_units + LANES), F32), shape((bc_units, LANES), F32)]
            tail_rows = 16 + 8 * (width // units)
            outs += [shape((w_rows + tail_rows, units), BF16)] * count
            res = call(
                partial(mixer_bwd_kernel, heads, count, mp, shared),
                "mixer_bwd",
                [
                    me, keep["normed"], keep["x_pre"], keep["bc_pre"], keep["stp"], dy, dgate,
                    wbc[layer], wdt[layer], cx[layer], cbc[layer], hp[layer], segm, segr,
                    gains[layer][None, :], ggn,
                ]
                + wz_p[layer]
                + wx_p[layer],
                outs,
                [
                    pltpu.VMEM((width, units), BF16),
                    pltpu.VMEM((width, units), BF16),
                    pltpu.VMEM((tokens, width), BF16),
                    pltpu.VMEM((width, units), BF16),
                    pltpu.VMEM((width, bc_units + LANES), F32),
                    pltpu.VMEM((bc_units, LANES), F32),
                    pltpu.VMEM((sm_rows, bc_units + LANES), F32),
                ],
                flops=16 << 30,
            )
            dn_parts = exchange(res[:mp], "mp")
            sm = res[mp : mp + (mp if shared else 2)]
            gx = res[mp + (mp if shared else 2) :]
            sm_parts = exchange(sm, "mp") if shared else []
            ins = [me] + dn_parts + sm_parts + [upstream, keep["hidden"], gains[layer][None, :]]
            outs = [shape((own, width), F32)]
            first = layer == 0
            if not first:
                ins += [saved[layer - 1]["branch"], saved[layer - 1]["gscale"]]
                outs += [shape((own, width + LANES), BF16)]
            scratch = []
            if shared:
                outs += [shape((sm_rows // count, bc_units + LANES), BF16)] * count
                scratch = [
                    pltpu.VMEM((sm_rows, bc_units + LANES), F32),
                    pltpu.VMEM((sm_rows // count, bc_units + LANES), F32),
                ]
            res = call(
                partial(after_bwd_kernel, first, mp, count, shared, float(inner)),
                "after_bwd",
                ins,
                outs,
                scratch,
                flops=1 << 28,
            )
            upstream = res[0]
            if not first:
                ext_p = spread(res[1], "mp")
            with jax.named_scope("sums"):
                if direct:
                    zo = add_up(exchange(zo_grads, "dp"))
                    gx = add_up(exchange(gx, "dp"))
                    sm = add_up(exchange(res[1 if first else 2 :], "dp"))
                    own_w = w_bc.shape[1]
                    g_wbc = sm[:own_w, :bc_units]
                    g_gain = sm[:own_w, bc_units] + sm[:own_w, bc_units + 1]
                    g_cbc = (sm[own_w:, :taps] + sm[own_w:, 8 : 8 + taps]).T
                    g_wz, g_wo = zo[:w_rows], zo[w_rows:].T
                    g_wx, tail = gx[:w_rows], gx[w_rows:]
                else:
                    def scattered(value):
                        return lax.psum_scatter(
                            value.astype(F32), "dp", scatter_dimension=0, tiled=True
                        )

                    g_wz = scattered(zo_grads[0][:width])
                    g_wo = scattered(zo_grads[0][width:]).T
                    g_wx = scattered(gx[0][:width])
                    tail = lax.psum(gx[0][width:].astype(F32), "dp")
                    gw = lax.psum_scatter(sm[0], ("dp", "mp"), scatter_dimension=0, tiled=True)
                    gc = lax.psum_scatter(sm[1], ("dp", "mp"), scatter_dimension=0, tiled=True)
                    g_wbc = gw[:, :bc_units]
                    g_gain = gw[:, bc_units] + gw[:, bc_units + 1]
                    g_cbc = (gc[:, :taps] + gc[:, 8 : 8 + taps]).T
                small = tail[:8] + tail[8:16]
                g_dt = jnp.concatenate(
                    [tail[16 + 8 * k : 24 + 8 * k] for k in range(width // units)], axis=1
                )
                g_dt = lax.dynamic_slice_in_dim(g_dt[:heads], my_dp * width_own, width_own, 1).T
                results[layer] = (
                    g_wz,
                    g_wx,
                    g_wbc,
                    g_dt,
                    g_wo,
                    small[:taps],
                    g_cbc,
                    small[6, :heads],
                    small[6, LANES : LANES + heads],
                    small[6, 2 * LANES : 2 * LANES + heads],
                    g_gain,
                    small[5],
                )
    stacked = [jnp.stack([results[i][m] for i in range(layers)]) for m in range(12)]
    return tuple([hidden, upstream] + stacked)


def solution(mesh):
    placed = (
        P(("dp", "mp"), None),
        P(None, "dp", "mp"),
        P(None, "dp", "mp"),
        P(None, ("dp", "mp"), None),
        P(None, "dp", "mp"),
        P(None, "mp", "dp"),
        P(None, None, "mp"),
        P(None, None, ("dp", "mp")),
        P(None, "mp"),
        P(None, "mp"),
        P(None, "mp"),
        P(None, ("dp", "mp")),
        P(None, "mp"),
        P("dp", None),
        P(("dp", "mp"), None),
    )
    return jax.shard_map(
        body,
        mesh=mesh,
        in_specs=placed,
        out_specs=(
            P(("dp", "mp"), None),
            P(("dp", "mp"), None),
            P(None, "dp", "mp"),
            P(None, "dp", "mp"),
            P(None, ("dp", "mp"), None),
            P(None, "dp", "mp"),
            P(None, "mp", "dp"),
            P(None, None, "mp"),
            P(None, None, ("dp", "mp")),
            P(None, "mp"),
            P(None, "mp"),
            P(None, "mp"),
            P(None, ("dp", "mp")),
            P(None, "mp"),
        ),
        check_vma=False,
    )
```

```python
from functools import partial

import jax
import jax.numpy as jnp
from jax import lax
from jax.experimental import pallas as pl
from jax.experimental.pallas import tpu as pltpu
from jax.sharding import PartitionSpec as P


GROUP = 128
LANES = 128
EPS = 1e-05
F32 = jnp.float32
BF16 = jnp.bfloat16
HIGH = lax.Precision.HIGHEST
INTERPRET = False


def mm(left, right):
    return jnp.dot(left, right, preferred_element_type=F32)


def mm_nt(left, right):
    return lax.dot_general(left, right, (((1,), (1,)), ((), ())), preferred_element_type=F32)


def mm_tn(left, right):
    return lax.dot_general(left, right, (((0,), (0,)), ((), ())), preferred_element_type=F32)


def high_low(value):
    high = value.astype(BF16)
    return high, (value - high.astype(F32)).astype(BF16)


def unit_map(heads, units):
    row = lax.broadcasted_iota(jnp.int32, (LANES, units), 0)
    col = lax.broadcasted_iota(jnp.int32, (LANES, units), 1)
    return jnp.where(row == col // (units // heads), 1.0, 0.0).astype(BF16)


def widen(per_head, umap):
    high, low = high_low(per_head)
    return mm(high, umap) + mm(low, umap)


def narrow(per_unit, umap):
    high, low = high_low(per_unit)
    return mm_nt(high, umap) + mm_nt(low, umap)


def sigmoid(value):
    return 1.0 / (1.0 + jnp.exp(-value))


def conv_sum(signal, taps, masks):
    total = taps[4:5] + taps[3:4] * signal
    for offset in range(1, 4):
        moved = pltpu.roll(signal, offset, 0)
        total = total + taps[3 - offset : 4 - offset] * (moved * masks[:, offset - 1 : offset])
    return total


def conv_back(d_act, pre, signal, taps, masks):
    rows = signal.shape[0]
    sg = sigmoid(pre)
    dc = d_act * (sg * (1.0 + pre * (1.0 - sg)))
    d_in = taps[3:4] * dc
    grads = {3: jnp.sum(dc * signal, axis=0, keepdims=True)}
    for offset in range(1, 4):
        masked = dc * masks[:, offset - 1 : offset]
        d_in = d_in + taps[3 - offset : 4 - offset] * pltpu.roll(masked, rows - offset, 0)
        grads[3 - offset] = jnp.sum(
            masked * pltpu.roll(signal, offset, 0), axis=0, keepdims=True
        )
    grads[4] = jnp.sum(dc, axis=0, keepdims=True)
    pad = jnp.zeros((3, signal.shape[1]), F32)
    return d_in, jnp.concatenate([grads[k] for k in range(5)] + [pad], axis=0)


def fill_rows(pieces, me, full):
    count = len(pieces)
    rows = pieces[0].shape[0]
    if count == 1:
        return pieces[0][...]
    for k, piece in enumerate(pieces):
        at = pl.multiple_of((me ^ k) * rows, rows)
        full[pl.ds(at, rows), :] = piece[...]
    return full[...]


def fill_stack(stack, begin, full):
    count = stack.shape[0]
    rows = full.shape[0] // count
    for d in range(count):
        full[d * rows : (d + 1) * rows, :] = stack[d, begin : begin + rows, :]
    return full[...]


def mixer_state(x_pre, bc_pre, stp, cx, cbc, hp, masks, heads):
    units = x_pre.shape[1]
    cols = bc_pre.shape[1] // 2
    rows = x_pre.shape[0]
    blocks = rows // GROUP
    umap = unit_map(heads, units)
    c_x = conv_sum(x_pre, cx, masks)
    c_bc = conv_sum(bc_pre, cbc, masks)
    x_act = c_x * sigmoid(c_x)
    bc_act = c_bc * sigmoid(c_bc)
    raw = stp + hp[0:1]
    step = jnp.maximum(raw, 0.0) + jnp.log1p(jnp.exp(-jnp.abs(raw)))
    rate = -step * jnp.exp(hp[1:2])
    pos_r = lax.broadcasted_iota(jnp.int32, (GROUP, GROUP), 0)
    pos_c = lax.broadcasted_iota(jnp.int32, (GROUP, GROUP), 1)
    lower = pos_r >= pos_c
    tri = jnp.where(lower, 1.0, 0.0)
    run = [
        jnp.dot(tri, rate[i * GROUP : (i + 1) * GROUP], precision=HIGH, preferred_element_type=F32)
        for i in range(blocks)
    ]
    u = [jnp.exp(r) for r in run]
    v = [jnp.exp(r[GROUP - 1 : GROUP] - r) for r in run]
    wide = widen(jnp.concatenate([step] + u + v + [jnp.broadcast_to(hp[2:3], (8, LANES))], axis=0), umap)
    step_u = wide[:rows]
    u_u = wide[rows : 2 * rows]
    v_u = wide[2 * rows : 3 * rows]
    skip_u = wide[3 * rows : 3 * rows + 1]
    b_bf = bc_act[:, :cols].astype(BF16)
    c_bf = bc_act[:, cols:].astype(BF16)
    xs = x_act * step_u
    return dict(
        umap=umap, c_x=c_x, c_bc=c_bc, x_act=x_act, raw=raw, step=step, rate=rate, lower=lower,
        tri=tri, run=run, step_u=step_u, u_u=u_u, v_u=v_u, skip_u=skip_u, b=b_bf, c=c_bf, xs=xs,
        blocks=blocks, heads=heads, units=units,
    )


def block_of(value, i):
    return value[i * GROUP : (i + 1) * GROUP]


def pair_lanes(heads, units):
    per = units // heads
    return LANES // per, per


def decay_tile(st, i, h, run_t):
    spread = st["run"][i][:, h : h + 1] - run_t[h : h + 1, :]
    return jnp.exp(jnp.where(st["keep"][i], spread, -1e30))


def scores_of(st, segc, segr, i):
    raw = mm_nt(block_of(st["c"], i), st["b"][: (i + 1) * GROUP])
    same = block_of(segc, i) == segr[:, : (i + 1) * GROUP]
    keep = same[:, i * GROUP :] & st["lower"]
    off = None
    if i:
        off = jnp.where(same[:, : i * GROUP], raw[:, : i * GROUP], 0.0)
    return off, raw[:, i * GROUP :], keep, same


def mixer_fwd_kernel(heads, *refs):
    nrm, wbc, wdt, cx, cbc, hp, segm, segr, wx = refs[:9]
    x_ref, bc_ref, st_ref, y_ref = refs[9:]
    normed = nrm[...]
    x_pre = mm(normed, wx[...])
    bc_pre = mm(normed, wbc[...])
    stp = mm(normed, wdt[...])
    x_ref[...] = x_pre
    bc_ref[...] = bc_pre
    st_ref[...] = stp
    masks = segm[...]
    segc, segl = masks[:, 3:4], segr[...]
    st = mixer_state(x_pre, bc_pre, stp, cx[...], cbc[...], hp[...], masks, heads)
    st["keep"] = {}
    units = st["units"]
    group, per = pair_lanes(heads, units)
    lane = lax.broadcasted_iota(jnp.int32, (GROUP, LANES), 1)
    xs_bf = st["xs"].astype(BF16)
    carried = []
    for i in range(st["blocks"]):
        off, diag, keep, _ = scores_of(st, segc, segl, i)
        st["keep"][i] = keep
        run_t = st["run"][i].T
        parts = []
        for p in range(units // LANES):
            x_pair = block_of(xs_bf, i)[:, p * LANES : (p + 1) * LANES]
            total = None
            for g in range(group):
                tile = (diag * decay_tile(st, i, p * group + g, run_t)).astype(BF16)
                part = mm(tile, x_pair)
                total = part if total is None else jnp.where(lane >= g * per, part, total)
            parts.append(total)
        y = jnp.concatenate(parts, axis=1) + st["skip_u"] * block_of(st["x_act"], i)
        u_i = block_of(st["u_u"], i)
        if i:
            held = jnp.concatenate([c.astype(BF16) for c in carried], axis=0)
            y = y + u_i * mm(off.astype(BF16), held)
        y_ref[i * GROUP : (i + 1) * GROUP, :] = y
        end = u_i[GROUP - 1 : GROUP]
        carried = [c * end for c in carried]
        carried.append(block_of(st["xs"], i) * block_of(st["v_u"], i))


def gate_fwd_kernel(last, mp_count, *refs):
    me, nrm, y, gg, zo = refs[:5]
    at = 5
    if last:
        cot_p = refs[at : at + mp_count]
        at += mp_count
    gate_ref = refs[at]
    outs = refs[at + 1 : at + 1 + mp_count]
    at += 1 + mp_count
    if last:
        stat_ref, dg_ref, up_ref = refs[at : at + 3]
        at += 3
    wz_s, wo_s, po_s = refs[at : at + 3]
    wz = fill_stack(zo, 0, wz_s)
    wo = fill_stack(zo, zo.shape[1] // 2, wo_s)
    gate = mm(nrm[...], wz)
    gate_ref[...] = gate
    mixed = y[...] * (gate * sigmoid(gate))
    weighted = mixed * gg[...]
    squares = jnp.sum(mixed * mixed, axis=1, keepdims=True)
    width = wo.shape[0]
    po_s[:, :width] = mm_nt(weighted.astype(BF16), wo).astype(BF16)
    high, low = high_low(squares)
    rows = squares.shape[0]
    lane = lax.broadcasted_iota(jnp.int32, (rows, LANES), 1)
    extra = jnp.where(lane == 0, high.astype(F32), jnp.where(lane == 1, low.astype(F32), 0.0))
    po_s[:, width:] = extra.astype(BF16)
    own = rows // mp_count
    for q in range(mp_count):
        begin = pl.multiple_of((me[1] ^ q) * own, own)
        outs[q][...] = po_s[pl.ds(begin, own), :]
    if last:
        ups = fill_rows(cot_p, me[1], up_ref)
        if mp_count == 1:
            up_ref[...] = ups
        dg = mm(ups, wo)
        dg_ref[...] = dg
        cross = jnp.sum(dg * weighted, axis=1, keepdims=True)
        stat = jnp.where(lane == 0, squares, jnp.where(lane == 1, cross, 0.0))
        stat_ref[...] = stat.T[:8, :]


def gate_bwd_kernel(last, count, mp_count, inner, *refs):
    me, nrm, y, gate, gg = refs[:5]
    at = 5
    if last:
        stats, dg_in, ups_ref = refs[at : at + 3]
        at += 3
    else:
        ups_p = refs[at : at + mp_count]
        at += mp_count
        zo = refs[at]
        at += 1
    dy_ref, dgate_ref, ggn_ref, out = refs[at : at + 4]
    at += 4
    scratch = refs[at:]
    rows = y.shape[0]
    width = nrm.shape[1]
    if last:
        total = stats[0]
        for k in range(1, stats.shape[0]):
            total = total + stats[k]
        pad = jnp.zeros((LANES - 8, rows), F32)
        cols = jnp.concatenate([total, pad], axis=0).T
        scale = lax.rsqrt(cols[:, 0:1] / inner + EPS)
        kappa = scale * scale * scale * cols[:, 1:2] / inner
        dg = dg_in[...]
        ups = ups_ref[...]
    else:
        ext = fill_rows(ups_p, me[1], scratch[0])
        tail = ext[:, width:].astype(F32)
        scale = tail[:, 0:1] + tail[:, 1:2]
        kappa = tail[:, 2:3] + tail[:, 3:4]
        ups = ext[:, :width]
        wo = fill_stack(zo, zo.shape[1] // 2, scratch[1])
        dg = mm(ups, wo)
    g = gate[...]
    sg = sigmoid(g)
    silu = g * sg
    mixed = y[...] * silu
    scaled = dg * scale
    ggn = jnp.sum(scaled * mixed, axis=0, keepdims=True)
    ggn_ref[...] = jnp.concatenate([ggn, jnp.zeros((7, ggn.shape[1]), F32)], axis=0)
    d_mixed = scaled * gg[...] - mixed * kappa
    d_gate = (d_mixed * y[...] * (sg * (1.0 + g * (1.0 - sg)))).astype(BF16)
    dgate_ref[...] = d_gate
    dy_ref[...] = d_mixed * silu
    gated = (mixed * scale * gg[...]).astype(BF16)
    g_wz = mm_tn(nrm[...], d_gate).astype(BF16)
    g_wo = mm_tn(ups, gated).astype(BF16)
    own = width // count
    for d in range(count):
        out[d, :own, :] = g_wz[d * own : (d + 1) * own]
        out[d, own:, :] = g_wo[d * own : (d + 1) * own]


def mixer_bwd_kernel(heads, count, mp_count, shared, *refs):
    me, nrm, xp, bp, sp, dy_in, dgate, wbc, wdt, cx, cbc, hp, segm, segr, gain, ggn = refs[:16]
    zo, wx = refs[16:18]
    at = 18
    dn_outs = refs[at : at + mp_count]
    at += mp_count
    if not shared:
        sm_outs = refs[at : at + 2]
        at += 2
    gx_out = refs[at]
    wz_s, dn_s, gw_s, gc_s, sm_s = refs[at + 1 : at + 6]
    x_pre, bc_pre, stp = xp[...], bp[...], sp[...]
    masks = segm[...]
    segc, segl = masks[:, 3:4], segr[...]
    st = mixer_state(x_pre, bc_pre, stp, cx[...], cbc[...], hp[...], masks, heads)
    st["keep"] = {}
    units, blocks, umap = st["units"], st["blocks"], st["umap"]
    group, per = pair_lanes(heads, units)
    lane = lax.broadcasted_iota(jnp.int32, (GROUP, LANES), 1)
    pos_r = lax.broadcasted_iota(jnp.int32, (GROUP, GROUP), 0)
    pos_c = lax.broadcasted_iota(jnp.int32, (GROUP, GROUP), 1)
    strict = pos_r > pos_c
    upper = jnp.where(pos_c >= pos_r, 1.0, 0.0)
    before = jnp.where(strict, 1.0, 0.0)
    dy = dy_in[...]
    xs_bf = st["xs"].astype(BF16)
    dy_bf = dy.astype(BF16)
    dyu = dy * st["u_u"]
    dyu_bf = dyu.astype(BF16)
    held = [[]]
    for i in range(blocks):
        end = block_of(st["u_u"], i)[GROUP - 1 : GROUP]
        new = [c * end for c in held[i]]
        new.append(block_of(st["xs"], i) * block_of(st["v_u"], i))
        held.append(new)
    later = None
    d_b = [None] * blocks
    d_c = [None] * blocks
    d_xs = [None] * blocks
    d_rate = [None] * blocks
    for i in reversed(range(blocks)):
        off, diag, keep, same = scores_of(st, segc, segl, i)
        st["keep"][i] = keep
        run_t = st["run"][i].T
        d_diag = None
        d_run = None
        parts = []
        for p in range(units // LANES):
            x_pair = block_of(xs_bf, i)[:, p * LANES : (p + 1) * LANES]
            dy_pair = block_of(dy_bf, i)[:, p * LANES : (p + 1) * LANES]
            total = None
            for g in range(group):
                h = p * group + g
                decay = decay_tile(st, i, h, run_t)
                tile = diag * decay
                mine = (lane >= g * per) & (lane < (g + 1) * per)
                d_tile = mm_nt(jnp.where(mine, dy_pair, jnp.zeros_like(dy_pair)), x_pair)
                part = mm_tn(tile.astype(BF16), dy_pair)
                total = part if total is None else jnp.where(lane >= g * per, part, total)
                term = d_tile * decay
                d_diag = term if d_diag is None else d_diag + term
                flow = jnp.where(strict, d_tile * tile, 0.0)
                high, low = high_low(flow)
                pick = jnp.where(pos_c == h, 1.0, 0.0).astype(BF16)
                turn = (mm(high, pick) + mm(low, pick)) - (mm_tn(high, pick) + mm_tn(low, pick))
                d_run = turn if d_run is None else d_run + turn
            parts.append(total)
        grad_xs = jnp.concatenate(parts, axis=1)
        d_scores = d_diag
        direct = None
        if i:
            rows_bf = block_of(dyu_bf, i)
            z_bf = jnp.concatenate([c.astype(BF16) for c in held[i]], axis=0)
            off_bf = off.astype(BF16)
            d_run = d_run + narrow(block_of(dyu, i) * mm(off_bf, z_bf), umap)
            d_off = jnp.where(same[:, : i * GROUP], mm_nt(rows_bf, z_bf), 0.0)
            d_scores = jnp.concatenate([d_off, d_diag], axis=1)
            direct = mm_tn(off_bf, rows_bf)
        rate_grad = jnp.dot(upper, d_run, precision=HIGH, preferred_element_type=F32)
        end = block_of(st["u_u"], i)[GROUP - 1 : GROUP]
        if later is not None:
            into = later[i]
            grad_xs = grad_xs + into * block_of(st["v_u"], i)
            q = narrow(into * held[i + 1][i], umap)
            rate_grad = rate_grad + jnp.dot(before, q, precision=HIGH, preferred_element_type=F32)
            if i:
                through = None
                for j in range(i):
                    part = jnp.sum(later[j] * held[i][j], axis=0, keepdims=True)
                    through = part if through is None else through + part
                through = jnp.broadcast_to(through * end, (8, units))
                rate_grad = rate_grad + narrow(through, umap)[0:1]
        new = []
        for j in range(i):
            term = direct[j * GROUP : (j + 1) * GROUP]
            if later is not None:
                term = term + later[j] * end
            new.append(term)
        later = new
        d_xs[i] = grad_xs
        d_rate[i] = rate_grad
        ds_bf = d_scores.astype(BF16)
        d_c[i] = mm(ds_bf, st["b"][: (i + 1) * GROUP])
        back = mm_tn(ds_bf, block_of(st["c"], i))
        for j in range(i + 1):
            term = back[j * GROUP : (j + 1) * GROUP]
            d_b[j] = term if d_b[j] is None else d_b[j] + term
    d_xs = jnp.concatenate(d_xs, axis=0)
    d_rate = jnp.concatenate(d_rate, axis=0)
    d_bc_act = jnp.concatenate(
        [jnp.concatenate(d_b, axis=0), jnp.concatenate(d_c, axis=0)], axis=1
    )
    d_x_act = d_xs * st["step_u"] + dy * st["skip_u"]
    d_step = narrow(d_xs * st["x_act"], umap) - d_rate * jnp.exp(hp[1:2, :])
    skip_row = jnp.broadcast_to(jnp.sum(dy * st["x_act"], axis=0, keepdims=True), (8, units))
    g_skip = narrow(skip_row, umap)[0:1]
    g_rate = jnp.sum(d_rate * st["rate"], axis=0, keepdims=True)
    d_stp = d_step * sigmoid(st["raw"])
    g_bias = jnp.sum(d_stp, axis=0, keepdims=True)
    head = lax.broadcasted_iota(jnp.int32, d_stp.shape, 1)
    d_stp_bf = jnp.where(head < heads, d_stp, 0.0).astype(BF16)
    d_x, g_cx = conv_back(d_x_act, st["c_x"], x_pre, cx[...], masks)
    d_bc, g_cbc = conv_back(d_bc_act, st["c_bc"], bc_pre, cbc[...], masks)
    d_x_bf = d_x.astype(BF16)
    d_bc_bf = d_bc.astype(BF16)
    wz = fill_stack(zo, 0, wz_s)
    dn = mm_nt(dgate[...], wz) + mm_nt(d_x_bf, wx[...])
    dn = dn + mm_nt(d_stp_bf, wdt[...]) + mm_nt(d_bc_bf, wbc[...])
    normed = nrm[...]
    hnorm = normed.astype(F32) / gain[...]
    g_gain = jnp.sum(dn * hnorm, axis=0, keepdims=True)
    width = normed.shape[1]
    rows = normed.shape[0]
    dn_s[...] = dn.astype(BF16)
    own = rows // mp_count
    for q in range(mp_count):
        begin = pl.multiple_of((me[1] ^ q) * own, own)
        dn_outs[q][:, :width] = dn_s[pl.ds(begin, own), :]
    bc_units = d_bc.shape[1]
    gw_s[:, :bc_units] = mm_tn(normed, d_bc_bf)
    g_high = g_gain.astype(BF16).astype(F32)
    gain_rows = jnp.concatenate([g_high, g_gain - g_high, jnp.zeros((LANES - 2, width), F32)], axis=0)
    gw_s[:, bc_units:] = gain_rows.T
    c_high = g_cbc.astype(BF16).astype(F32)
    conv_rows = jnp.concatenate([c_high, g_cbc - c_high, jnp.zeros((LANES - 16, bc_units), F32)], axis=0)
    gc_s[...] = conv_rows.T
    if shared:
        w_own = width // (shared * mp_count)
        c_own = bc_units // (shared * mp_count)
        for q in range(mp_count):
            for k in range(shared):
                slot = k * mp_count + (me[1] ^ q)
                sm_s[k * w_own : (k + 1) * w_own, :] = gw_s[
                    pl.ds(pl.multiple_of(slot * w_own, w_own), w_own), :
                ]
                base = shared * w_own + k * c_own
                sm_s[base : base + c_own, :LANES] = gc_s[
                    pl.ds(pl.multiple_of(slot * c_own, c_own), c_own), :
                ]
                sm_s[base : base + c_own, LANES:] = jnp.zeros((c_own, bc_units), F32)
            half = sm_s.shape[0] // 2
            sm_cols = sm_s.shape[1]
            dn_outs[q][:, width : width + sm_cols] = sm_s[:half, :].astype(BF16)
            dn_outs[q][:, width + sm_cols :] = sm_s[half:, :].astype(BF16)
    else:
        sm_outs[0][...] = gw_s[...]
        sm_outs[1][...] = gc_s[...]
    g_wx = mm_tn(normed, d_x_bf).astype(BF16)
    heads_row = jnp.concatenate([g_bias, g_rate, g_skip], axis=1)
    if heads_row.shape[1] < units:
        heads_row = jnp.concatenate(
            [heads_row, jnp.zeros((1, units - heads_row.shape[1]), F32)], axis=1
        )
    small = jnp.concatenate([g_cx[:5], ggn[0:1, :], heads_row, jnp.zeros((1, units), F32)], axis=0)
    s_high, s_low = high_low(small)
    g_dt = mm_tn(d_stp_bf, normed)[:8]
    halves = [g_dt[:, k * units : (k + 1) * units] for k in range(width // units)]
    tail = jnp.concatenate([s_high.astype(F32), s_low.astype(F32)] + halves, axis=0).astype(BF16)
    own = width // count
    for d in range(count):
        gx_out[d, :own, :] = g_wx[d * own : (d + 1) * own]
        gx_out[d, own:, :] = tail


def after_fwd_kernel(last, mp_count, inner, *refs):
    parts = refs[:mp_count]
    hidden, gain = refs[mp_count : mp_count + 2]
    outs = refs[mp_count + 2 :]
    total = parts[0][...].astype(F32)
    for part in parts[1:]:
        total = total + part[...].astype(F32)
    width = hidden.shape[1]
    squares = total[:, width : width + 1] + total[:, width + 1 : width + 2]
    scale = lax.rsqrt(squares / inner + EPS)
    branch = total[:, :width] * scale
    new = hidden[...] + branch
    outs[0][...] = new
    if not last:
        norm = lax.rsqrt(jnp.mean(new * new, axis=1, keepdims=True) + EPS)
        outs[1][...] = (new * norm * gain[...]).astype(BF16)
        outs[2][...] = branch
        outs[3][...] = scale


def after_bwd_kernel(first, mp_count, count, shared, inner, *refs):
    parts = refs[:mp_count]
    at = mp_count
    ups, hidden, gain = refs[at : at + 3]
    at += 3
    if not first:
        branch, gscale = refs[at : at + 2]
        at += 2
    up_ref = refs[at]
    at += 1
    if not first:
        ext_ref = refs[at]
        at += 1
    h = hidden[...]
    width = h.shape[1]
    dn = parts[0][:, :width].astype(F32)
    for part in parts[1:]:
        dn = dn + part[:, :width].astype(F32)
    scale = lax.rsqrt(jnp.mean(h * h, axis=1, keepdims=True) + EPS)
    hnorm = h * scale
    dh = dn * gain[...]
    new = ups[...] + scale * (dh - hnorm * jnp.mean(dh * hnorm, axis=1, keepdims=True))
    up_ref[...] = new
    if not first:
        rounded = new.astype(BF16)
        gs = gscale[...]
        dot = jnp.sum(rounded.astype(F32) * branch[...], axis=1, keepdims=True)
        kappa = gs * gs * dot / inner
        lane = lax.broadcasted_iota(jnp.int32, (h.shape[0], LANES), 1)
        s_high, s_low = high_low(gs)
        k_high, k_low = high_low(kappa)
        extra = jnp.zeros((h.shape[0], LANES), F32)
        for at_lane, col in enumerate((s_high, s_low, k_high, k_low)):
            extra = jnp.where(lane == at_lane, col.astype(F32), extra)
        ext_ref[:, :width] = rounded
        ext_ref[:, width:] = extra.astype(BF16)
    if shared:
        sm_out, total_s, mix_s = refs[at : at + 3]
        cols = total_s.shape[1]
        total = parts[0][:, width:].astype(F32)
        for part in parts[1:]:
            total = total + part[:, width:].astype(F32)
        total = jnp.concatenate([total[:, :cols], total[:, cols:]], axis=0)
        bc_units = total.shape[1] - LANES
        w_rows = gain.shape[1] // mp_count
        w_own = w_rows // count
        c_own = (total.shape[0] - w_rows) // count
        tail = total[:w_rows, bc_units:]
        lane = lax.broadcasted_iota(jnp.int32, tail.shape, 1)
        joined = tail[:, 0:1] + tail[:, 1:2]
        j_high = joined.astype(BF16).astype(F32)
        total_s[:w_rows, :bc_units] = total[:w_rows, :bc_units]
        total_s[:w_rows, bc_units:] = jnp.where(
            lane == 0, j_high, jnp.where(lane == 1, joined - j_high, 0.0)
        )
        conv = total[w_rows:, :LANES]
        lane = lax.broadcasted_iota(jnp.int32, conv.shape, 1)
        joined = jnp.where(lane < 8, conv + pltpu.roll(conv, LANES - 8, 1), 0.0)
        j_high = joined.astype(BF16).astype(F32)
        total_s[w_rows:, :LANES] = j_high + pltpu.roll(joined - j_high, 8, 1)
        total_s[w_rows:, LANES:] = jnp.zeros((total.shape[0] - w_rows, bc_units), F32)
        for d in range(count):
            mix_s[:w_own, :] = total_s[d * w_own : (d + 1) * w_own, :]
            mix_s[w_own:, :] = total_s[w_rows + d * c_own : w_rows + (d + 1) * c_own, :]
            sm_out[d] = mix_s[...].astype(BF16)


def place_kernel(*refs):
    me, pieces, (wx_ref, sm_ref) = refs[0], refs[1:-2], refs[-2:]
    rows = wx_ref.shape[0] // len(pieces)
    half = rows // 2
    left = pieces[0].shape[1]
    rest = wx_ref.shape[1] - left
    sm_rows = pieces[0].shape[0] - rows - half
    for k, piece in enumerate(pieces):
        at = pl.multiple_of((me[0] ^ k) * rows, half)
        below = pl.multiple_of(at + half, half)
        wx_ref[pl.ds(at, rows), :left] = piece[:rows, :]
        wx_ref[pl.ds(at, half), left:] = piece[rows : rows + half, :rest]
        wx_ref[pl.ds(below, half), left:] = piece[rows : rows + half, rest:]
        at = pl.multiple_of((me[0] ^ k) * sm_rows, sm_rows)
        sm_ref[pl.ds(at, sm_rows), :] = piece[rows + half :, :]


def small_kernel(layers, taps, dt_groups, own_w, *refs):
    every, mine, hs = refs[:3]
    wbc_ref, wdt_ref, gain_ref, cbc_ref, nrm_ref = refs[3:8]
    w_s, g_s, c_s, d_s = refs[8:]
    mp_count = every.shape[0]
    dp_count = mine.shape[0] // (layers * (own_w + 8))
    for layer in range(layers):
        d_s[...] = jnp.zeros(d_s.shape, F32)
        for d in range(dp_count):
            base = (d * layers + layer) * (own_w + 8)
            for m in range(mp_count):
                slot = d * mp_count + m
                w_s[slot * own_w : (slot + 1) * own_w, :] = every[m, base : base + own_w, :].astype(F32)
                tile = every[m, base + own_w - 8 : base + own_w + 8, :LANES].astype(F32)[8:]
                c_s[slot * 8 : slot * 8 + 8, :] = tile
                for c in range(own_w // 8):
                    row = slot * own_w + 8 * c
                    g_s[row : row + 8, :] = pltpu.roll(tile, LANES - 8 - c, 1)
            tile = mine[base + own_w - 8 : base + own_w + 8, :LANES].astype(F32)[8:]
            for g in range(dt_groups):
                row = (d * dt_groups + g) * 8
                d_s[row : row + 8, :] = pltpu.roll(tile, LANES - 16 - 8 * g, 1)
        wbc_ref[layer] = w_s[...].astype(BF16)
        lane = lax.broadcasted_iota(jnp.int32, d_s.shape, 1)
        wdt_ref[layer] = jnp.where(lane < 8, d_s[...], 0.0).astype(BF16)
        gain = g_s[...].T[:8]
        gain_ref[layer] = gain
        conv = c_s[...].T[:8]
        row = lax.broadcasted_iota(jnp.int32, conv.shape, 0)
        cbc_ref[layer] = jnp.where(row < taps, conv, 0.0)
        if layer == 0:
            nrm_ref[...] = (hs[...].astype(F32) * gain[0:1]).astype(BF16)


def call(kernel, name, inputs, outputs, scratch=(), flops=1 << 28):
    specs = []
    for value in inputs:
        space = pltpu.SMEM if value.dtype == jnp.int32 and value.ndim == 1 else pltpu.VMEM
        specs.append(pl.BlockSpec(memory_space=space))
    size = sum(v.size * v.dtype.itemsize for v in inputs)
    size += sum(v.size * v.dtype.itemsize for v in outputs)
    return pl.pallas_call(
        kernel,
        out_shape=[jax.ShapeDtypeStruct(o.shape, o.dtype) for o in outputs],
        in_specs=specs,
        out_specs=[pl.BlockSpec(memory_space=pltpu.VMEM) for _ in outputs],
        scratch_shapes=list(scratch),
        cost_estimate=pl.CostEstimate(flops=flops, bytes_accessed=size, transcendentals=0),
        compiler_params=pltpu.CompilerParams(vmem_limit_bytes=60 << 20),
        interpret=INTERPRET,
        name=name,
    )(*inputs)


def shape(dims, dtype):
    return jax.ShapeDtypeStruct(tuple(dims), dtype)


def partners(axis, k):
    return [(i, i ^ k) for i in range(lax.axis_size(axis))]


def spread(value, axis):
    n = lax.axis_size(axis)
    return [value] + [lax.ppermute(value, axis, partners(axis, k)) for k in range(1, n)]


def exchange(values, axis):
    n = lax.axis_size(axis)
    return [values[0]] + [lax.ppermute(values[k], axis, partners(axis, k)) for k in range(1, n)]


def share(value, axis):
    n = lax.axis_size(axis)
    return lax.all_to_all(jnp.broadcast_to(value[None], (n,) + value.shape), axis, 0, 0)


def swap(stack, axis):
    return lax.all_to_all(stack, axis, 0, 0)


def add_up(stack):
    return jnp.sum(stack.astype(F32), axis=0)


def body(
    h_in,
    w_z,
    w_x,
    w_bc,
    w_dt,
    w_out,
    conv_x,
    conv_bc,
    dt_bias,
    a_log,
    d_skip,
    rms_gain,
    gnorm_gain,
    seg_ids,
    cotangent,
):
    dp, mp = lax.axis_size("dp"), lax.axis_size("mp")
    direct = dp & (dp - 1) == 0 and conv_bc.shape[2] == 8 and w_bc.shape[1] == 24
    layers, width_own, units = w_z.shape
    width = h_in.shape[1]
    tokens = h_in.shape[0] * mp
    own = h_in.shape[0]
    heads = w_dt.shape[2]
    bc_units = w_bc.shape[2]
    taps = conv_x.shape[1]
    inner = units * mp
    my_dp, my_mp = lax.axis_index("dp"), lax.axis_index("mp")
    me = jnp.stack([my_dp if direct else jnp.zeros_like(my_dp), my_mp]).astype(jnp.int32)
    count = dp if direct else 1
    w_rows = width // count

    out_t = jnp.swapaxes(w_out, 1, 2)
    hidden = h_in
    scale = lax.rsqrt(jnp.mean(h_in * h_in, axis=1, keepdims=True) + EPS)
    scaled = (h_in * scale).astype(BF16)
    wx_full, zo_full = [], []
    if direct:
        own_w = w_bc.shape[1]
        own_c = conv_bc.shape[2]
        groups = width_own // 8
        dt = jnp.pad(w_dt, ((0, 0), (0, 0), (0, 8 - heads))).reshape(layers, groups, 8, 8)
        dt = jnp.swapaxes(dt, 1, 2).reshape(layers, 8, groups * 8)
        gain = jnp.swapaxes(rms_gain.reshape(layers, own_w // 8, 8), 1, 2)
        conv = jnp.pad(jnp.swapaxes(conv_bc, 1, 2), ((0, 0), (0, 0), (0, 8 - taps)))
        low = jnp.concatenate([conv, jnp.pad(gain, ((0, 0), (0, 0), (0, 8 - own_w // 8))), dt], axis=2)
        low = jnp.pad(low, ((0, 0), (0, 0), (0, bc_units - low.shape[2])))
        packed = jnp.concatenate([w_bc, low], axis=1).reshape(-1, bc_units)
        half = width_own // 2
        first = w_x[0]
        group = jnp.concatenate(
            [
                first[:, :bc_units],
                jnp.concatenate([first[:half, bc_units:], first[half:, bc_units:]], axis=1),
                packed,
            ],
            axis=0,
        )
        pieces = spread(group, "dp")
        wx0, mine = call(
            place_kernel,
            "place",
            [me] + pieces,
            [shape((width, units), BF16), shape((dp * packed.shape[0], bc_units), BF16)],
        )
        wx_full.append(wx0)
        hs = lax.all_gather(scaled, "mp", axis=0, tiled=True)
        every = lax.all_gather(mine, "mp", axis=0)
        wbc, wdt, gains, cbc, normed = call(
            partial(small_kernel, layers, taps, groups, own_w),
            "small",
            [every, mine, hs],
            [
                shape((layers, width, bc_units), BF16),
                shape((layers, width, LANES), BF16),
                shape((layers, 8, width), F32),
                shape((layers, 8, bc_units), F32),
                shape((tokens, width), BF16),
            ],
            [
                pltpu.VMEM((width, bc_units), F32),
                pltpu.VMEM((width, LANES), F32),
                pltpu.VMEM((bc_units, LANES), F32),
                pltpu.VMEM((width, LANES), F32),
            ],
        )
        gains = gains[:, 0]
        for layer in range(layers):
            if layer:
                wx_full.append(share(w_x[layer], "dp").reshape(width, units))
            zo_full.append(share(jnp.concatenate([w_z[layer], out_t[layer]], axis=0), "dp"))
    else:
        both = ("dp", "mp")
        wbc = lax.all_gather(w_bc, both, axis=1, tiled=True)
        gains = lax.all_gather(rms_gain, both, axis=1, tiled=True).astype(F32)
        cbc = lax.all_gather(conv_bc, both, axis=2, tiled=True).astype(F32)
        cbc = jnp.pad(cbc, ((0, 0), (0, 8 - taps), (0, 0)))
        wdt = lax.all_gather(w_dt, "dp", axis=1, tiled=True)
        wdt = jnp.pad(wdt, ((0, 0), (0, 0), (0, LANES - heads)))
        for layer in range(layers):
            wx_full.append(lax.all_gather(w_x[layer], "dp", axis=0, tiled=True))
            pair = [
                lax.all_gather(value, "dp", axis=0, tiled=True)
                for value in (w_z[layer], out_t[layer])
            ]
            zo_full.append(jnp.concatenate(pair, axis=0)[None])
        hs = lax.all_gather(scaled, "mp", axis=0, tiled=True)
        normed = (hs.astype(F32) * gains[0][None, :]).astype(BF16)

    segment = seg_ids[0]
    seg_f = segment.astype(F32)
    cols = []
    for offset in range(1, 4):
        earlier = jnp.concatenate([jnp.full((offset,), -1, jnp.int32), segment[:-offset]])
        cols.append((earlier == segment).astype(F32))
    segm = jnp.stack(cols + [seg_f], axis=1)
    segr = seg_f[None, :]
    hp = jnp.stack([dt_bias, a_log, d_skip], axis=1)
    hp = jnp.pad(hp, ((0, 0), (0, 5), (0, LANES - heads)))
    cx = jnp.pad(conv_x, ((0, 0), (0, 8 - taps), (0, 0)))

    cot_p = spread(cotangent.astype(BF16), "mp")

    saved = []
    for layer in range(layers):
        last = layer == layers - 1
        with jax.named_scope(f"fwd_{layer}"):
            x_pre, bc_pre, stp, y = call(
                partial(mixer_fwd_kernel, heads),
                "mixer_fwd",
                [normed, wbc[layer], wdt[layer], cx[layer], cbc[layer], hp[layer], segm, segr]
                + [wx_full[layer]],
                [
                    shape((tokens, units), F32),
                    shape((tokens, bc_units), F32),
                    shape((tokens, LANES), F32),
                    shape((tokens, units), F32),
                ],
                flops=8 << 30,
            )
            gg = gnorm_gain[layer][None, :]
            outs = [shape((tokens, units), F32)]
            outs += [shape((own, width + LANES), BF16)] * mp
            ins = [me, normed, y, gg, zo_full[layer]]
            if last:
                ins += cot_p
                outs += [
                    shape((8, tokens), F32),
                    shape((tokens, units), F32),
                    shape((tokens, width), BF16),
                ]
            res = call(
                partial(gate_fwd_kernel, last, mp),
                "gate_fwd",
                ins,
                outs,
                [
                    pltpu.VMEM((width, units), BF16),
                    pltpu.VMEM((width, units), BF16),
                    pltpu.VMEM((tokens, width + LANES), BF16),
                ],
                flops=4 << 30,
            )
            gate, parts = res[0], res[1 : 1 + mp]
            if last:
                stats = lax.all_gather(res[1 + mp], "mp", axis=0)
                dg, ups_bf = res[2 + mp], res[3 + mp]
            got = exchange(parts, "mp")
            keep = dict(hidden=hidden, normed=normed, x_pre=x_pre, bc_pre=bc_pre, stp=stp, y=y, gate=gate, gg=gg)
            nxt = gains[min(layer + 1, layers - 1)][None, :]
            outs = [shape((own, width), F32)]
            if not last:
                outs += [
                    shape((own, width), BF16),
                    shape((own, width), F32),
                    shape((own, 1), F32),
                ]
            res = call(
                partial(after_fwd_kernel, last, mp, float(inner)),
                "after_fwd",
                got + [hidden, nxt],
                outs,
                flops=1 << 28,
            )
            hidden = res[0]
            if not last:
                keep["branch"], keep["gscale"] = res[2], res[3]
                normed = lax.all_gather(res[1], "mp", axis=0, tiled=True)
            saved.append(keep)

    upstream = cotangent
    results = [None] * layers
    ext_p = None
    for layer in reversed(range(layers)):
        last = layer == layers - 1
        keep = saved[layer]
        with jax.named_scope(f"bwd_{layer}"):
            ins = [me, keep["normed"], keep["y"], keep["gate"], keep["gg"]]
            scratch = []
            if last:
                ins += [stats, dg, ups_bf]
            else:
                ins += ext_p + [zo_full[layer]]
                scratch += [
                    pltpu.VMEM((tokens, width + LANES), BF16),
                    pltpu.VMEM((width, units), BF16),
                ]
            res = call(
                partial(gate_bwd_kernel, last, count, mp, float(inner)),
                "gate_bwd",
                ins,
                [
                    shape((tokens, units), F32),
                    shape((tokens, units), BF16),
                    shape((8, units), F32),
                ]
                + [shape((count, 2 * w_rows, units), BF16)],
                scratch,
                flops=6 << 30,
            )
            dy, dgate, ggn, zo_grads = res
            shared = dp if direct else 0
            sm_rows = (width + bc_units) // mp
            sm_width = sm_rows // 2 // own * 2 * (bc_units + LANES) if shared else 0
            outs = [shape((own, width + sm_width), BF16)] * mp
            if not shared:
                outs += [shape((width, bc_units + LANES), F32), shape((bc_units, LANES), F32)]
            tail_rows = 16 + 8 * (width // units)
            outs += [shape((count, w_rows + tail_rows, units), BF16)]
            res = call(
                partial(mixer_bwd_kernel, heads, count, mp, shared),
                "mixer_bwd",
                [
                    me, keep["normed"], keep["x_pre"], keep["bc_pre"], keep["stp"], dy, dgate,
                    wbc[layer], wdt[layer], cx[layer], cbc[layer], hp[layer], segm, segr,
                    gains[layer][None, :], ggn, zo_full[layer], wx_full[layer],
                ],
                outs,
                [
                    pltpu.VMEM((width, units), BF16),
                    pltpu.VMEM((tokens, width), BF16),
                    pltpu.VMEM((width, bc_units + LANES), F32),
                    pltpu.VMEM((bc_units, LANES), F32),
                    pltpu.VMEM((sm_rows, bc_units + LANES), F32),
                ],
                flops=16 << 30,
            )
            dn_parts = exchange(res[:mp], "mp")
            sm, gx = res[mp:-1], res[-1]
            ins = dn_parts + [upstream, keep["hidden"], gains[layer][None, :]]
            outs = [shape((own, width), F32)]
            first = layer == 0
            if not first:
                ins += [saved[layer - 1]["branch"], saved[layer - 1]["gscale"]]
                outs += [shape((own, width + LANES), BF16)]
            scratch = []
            if shared:
                outs += [shape((count, sm_rows // count, bc_units + LANES), BF16)]
                scratch = [
                    pltpu.VMEM((sm_rows, bc_units + LANES), F32),
                    pltpu.VMEM((sm_rows // count, bc_units + LANES), F32),
                ]
            res = call(
                partial(after_bwd_kernel, first, mp, count, shared, float(inner)),
                "after_bwd",
                ins,
                outs,
                scratch,
                flops=1 << 28,
            )
            upstream = res[0]
            if not first:
                ext_p = spread(res[1], "mp")
            with jax.named_scope("sums"):
                if direct:
                    zo = add_up(swap(zo_grads, "dp"))
                    gx = add_up(swap(gx, "dp"))
                    sm = add_up(swap(res[-1], "dp"))
                    own_w = w_bc.shape[1]
                    g_wbc = sm[:own_w, :bc_units]
                    g_gain = sm[:own_w, bc_units] + sm[:own_w, bc_units + 1]
                    g_cbc = (sm[own_w:, :taps] + sm[own_w:, 8 : 8 + taps]).T
                    g_wz, g_wo = zo[:w_rows], zo[w_rows:].T
                    g_wx, tail = gx[:w_rows], gx[w_rows:]
                else:
                    def scattered(value):
                        return lax.psum_scatter(
                            value.astype(F32), "dp", scatter_dimension=0, tiled=True
                        )

                    g_wz = scattered(zo_grads[0, :width])
                    g_wo = scattered(zo_grads[0, width:]).T
                    g_wx = scattered(gx[0, :width])
                    tail = lax.psum(gx[0, width:].astype(F32), "dp")
                    gw = lax.psum_scatter(sm[0], ("dp", "mp"), scatter_dimension=0, tiled=True)
                    gc = lax.psum_scatter(sm[1], ("dp", "mp"), scatter_dimension=0, tiled=True)
                    g_wbc = gw[:, :bc_units]
                    g_gain = gw[:, bc_units] + gw[:, bc_units + 1]
                    g_cbc = (gc[:, :taps] + gc[:, 8 : 8 + taps]).T
                small = tail[:8] + tail[8:16]
                g_dt = jnp.concatenate(
                    [tail[16 + 8 * k : 24 + 8 * k] for k in range(width // units)], axis=1
                )
                g_dt = lax.dynamic_slice_in_dim(g_dt[:heads], my_dp * width_own, width_own, 1).T
                results[layer] = (
                    g_wz,
                    g_wx,
                    g_wbc,
                    g_dt,
                    g_wo,
                    small[:taps],
                    g_cbc,
                    small[6, :heads],
                    small[6, LANES : LANES + heads],
                    small[6, 2 * LANES : 2 * LANES + heads],
                    g_gain,
                    small[5],
                )
    stacked = [jnp.stack([results[i][m] for i in range(layers)]) for m in range(12)]
    return tuple([hidden, upstream] + stacked)


def solution(mesh):
    placed = (
        P(("dp", "mp"), None),
        P(None, "dp", "mp"),
        P(None, "dp", "mp"),
        P(None, ("dp", "mp"), None),
        P(None, "dp", "mp"),
        P(None, "mp", "dp"),
        P(None, None, "mp"),
        P(None, None, ("dp", "mp")),
        P(None, "mp"),
        P(None, "mp"),
        P(None, "mp"),
        P(None, ("dp", "mp")),
        P(None, "mp"),
        P("dp", None),
        P(("dp", "mp"), None),
    )
    return jax.shard_map(
        body,
        mesh=mesh,
        in_specs=placed,
        out_specs=(
            P(("dp", "mp"), None),
            P(("dp", "mp"), None),
            P(None, "dp", "mp"),
            P(None, "dp", "mp"),
            P(None, ("dp", "mp"), None),
            P(None, "dp", "mp"),
            P(None, "mp", "dp"),
            P(None, None, "mp"),
            P(None, None, ("dp", "mp")),
            P(None, "mp"),
            P(None, "mp"),
            P(None, "mp"),
            P(None, ("dp", "mp")),
            P(None, "mp"),
        ),
        check_vma=False,
    )
```

```python
from functools import partial

import jax
import jax.numpy as jnp
from jax import lax
from jax.experimental import pallas as pl
from jax.experimental.pallas import tpu as pltpu
from jax.sharding import PartitionSpec as P


GROUP = 128
LANES = 128
EPS = 1e-05
F32 = jnp.float32
BF16 = jnp.bfloat16
HIGH = lax.Precision.HIGHEST
INTERPRET = False


def mm(left, right):
    return jnp.dot(left, right, preferred_element_type=F32)


def mm_nt(left, right):
    return lax.dot_general(left, right, (((1,), (1,)), ((), ())), preferred_element_type=F32)


def mm_tn(left, right):
    return lax.dot_general(left, right, (((0,), (0,)), ((), ())), preferred_element_type=F32)


def high_low(value):
    high = value.astype(BF16)
    return high, (value - high.astype(F32)).astype(BF16)


def unit_map(heads, units):
    row = lax.broadcasted_iota(jnp.int32, (LANES, units), 0)
    col = lax.broadcasted_iota(jnp.int32, (LANES, units), 1)
    return jnp.where(row == col // (units // heads), 1.0, 0.0).astype(BF16)


def widen(per_head, umap):
    high, low = high_low(per_head)
    return mm(high, umap) + mm(low, umap)


def narrow(per_unit, umap):
    high, low = high_low(per_unit)
    return mm_nt(high, umap) + mm_nt(low, umap)


def sigmoid(value):
    return 1.0 / (1.0 + jnp.exp(-value))


def conv_sum(signal, taps, masks):
    total = taps[4:5] + taps[3:4] * signal
    for offset in range(1, 4):
        moved = pltpu.roll(signal, offset, 0)
        total = total + taps[3 - offset : 4 - offset] * (moved * masks[:, offset - 1 : offset])
    return total


def conv_back(d_act, pre, signal, taps, masks):
    rows = signal.shape[0]
    sg = sigmoid(pre)
    dc = d_act * (sg * (1.0 + pre * (1.0 - sg)))
    d_in = taps[3:4] * dc
    grads = {3: jnp.sum(dc * signal, axis=0, keepdims=True)}
    for offset in range(1, 4):
        masked = dc * masks[:, offset - 1 : offset]
        d_in = d_in + taps[3 - offset : 4 - offset] * pltpu.roll(masked, rows - offset, 0)
        grads[3 - offset] = jnp.sum(
            masked * pltpu.roll(signal, offset, 0), axis=0, keepdims=True
        )
    grads[4] = jnp.sum(dc, axis=0, keepdims=True)
    pad = jnp.zeros((3, signal.shape[1]), F32)
    return d_in, jnp.concatenate([grads[k] for k in range(5)] + [pad], axis=0)


def fill_rows(pieces, me, full):
    count = len(pieces)
    rows = pieces[0].shape[0]
    if count == 1:
        return pieces[0][...]
    for k, piece in enumerate(pieces):
        at = pl.multiple_of((me ^ k) * rows, rows)
        full[pl.ds(at, rows), :] = piece[...]
    return full[...]


def fill_stack(stack, begin, full):
    count = stack.shape[0]
    rows = full.shape[0] // count
    for d in range(count):
        full[d * rows : (d + 1) * rows, :] = stack[d, begin : begin + rows, :]
    return full[...]


def mixer_state(x_pre, bc_pre, stp, cx, cbc, hp, masks, heads):
    units = x_pre.shape[1]
    cols = bc_pre.shape[1] // 2
    rows = x_pre.shape[0]
    blocks = rows // GROUP
    umap = unit_map(heads, units)
    c_x = conv_sum(x_pre, cx, masks)
    c_bc = conv_sum(bc_pre, cbc, masks)
    x_act = c_x * sigmoid(c_x)
    bc_act = c_bc * sigmoid(c_bc)
    raw = stp + hp[0:1]
    step = jnp.maximum(raw, 0.0) + jnp.log1p(jnp.exp(-jnp.abs(raw)))
    rate = -step * jnp.exp(hp[1:2])
    pos_r = lax.broadcasted_iota(jnp.int32, (GROUP, GROUP), 0)
    pos_c = lax.broadcasted_iota(jnp.int32, (GROUP, GROUP), 1)
    lower = pos_r >= pos_c
    tri = jnp.where(lower, 1.0, 0.0)
    run = [
        jnp.dot(tri, rate[i * GROUP : (i + 1) * GROUP], precision=HIGH, preferred_element_type=F32)
        for i in range(blocks)
    ]
    u = [jnp.exp(r) for r in run]
    v = [jnp.exp(r[GROUP - 1 : GROUP] - r) for r in run]
    wide = widen(jnp.concatenate([step] + u + v + [jnp.broadcast_to(hp[2:3], (8, LANES))], axis=0), umap)
    step_u = wide[:rows]
    u_u = wide[rows : 2 * rows]
    v_u = wide[2 * rows : 3 * rows]
    skip_u = wide[3 * rows : 3 * rows + 1]
    b_bf = bc_act[:, :cols].astype(BF16)
    c_bf = bc_act[:, cols:].astype(BF16)
    xs = x_act * step_u
    return dict(
        umap=umap, c_x=c_x, c_bc=c_bc, x_act=x_act, raw=raw, step=step, rate=rate, lower=lower,
        tri=tri, run=run, step_u=step_u, u_u=u_u, v_u=v_u, skip_u=skip_u, b=b_bf, c=c_bf, xs=xs,
        blocks=blocks, heads=heads, units=units,
    )


def block_of(value, i):
    return value[i * GROUP : (i + 1) * GROUP]


def pair_lanes(heads, units):
    per = units // heads
    return LANES // per, per


def decay_tile(st, i, h, run_t):
    spread = st["run"][i][:, h : h + 1] - run_t[h : h + 1, :]
    return jnp.exp(jnp.where(st["keep"][i], spread, -1e30))


def scores_of(st, segc, segr, i):
    raw = mm_nt(block_of(st["c"], i), st["b"][: (i + 1) * GROUP])
    same = block_of(segc, i) == segr[:, : (i + 1) * GROUP]
    keep = same[:, i * GROUP :] & st["lower"]
    off = None
    if i:
        off = jnp.where(same[:, : i * GROUP], raw[:, : i * GROUP], 0.0)
    return off, raw[:, i * GROUP :], keep, same


def mixer_fwd_kernel(heads, mp_count, w_count, *refs):
    me, wbc, wdt, cx, cbc, hp, segm, segr = refs[:8]
    nrm = refs[8 : 8 + mp_count]
    at = 8 + mp_count
    wx_p = refs[at : at + w_count]
    at += w_count
    x_ref, bc_ref, st_ref, y_ref = refs[at : at + 4]
    at += 4
    if mp_count > 1:
        normed = fill_rows(nrm, me[1], refs[at])
        at += 1
    else:
        normed = nrm[0][...]
    wx = fill_rows(wx_p, me[0], refs[at]) if w_count > 1 else wx_p[0][...]
    x_pre = mm(normed, wx)
    bc_pre = mm(normed, wbc[...])
    stp = mm(normed, wdt[...])
    x_ref[...] = x_pre
    bc_ref[...] = bc_pre
    st_ref[...] = stp
    masks = segm[...]
    segc, segl = masks[:, 3:4], segr[...]
    st = mixer_state(x_pre, bc_pre, stp, cx[...], cbc[...], hp[...], masks, heads)
    st["keep"] = {}
    units = st["units"]
    group, per = pair_lanes(heads, units)
    lane = lax.broadcasted_iota(jnp.int32, (GROUP, LANES), 1)
    xs_bf = st["xs"].astype(BF16)
    carried = []
    for i in range(st["blocks"]):
        off, diag, keep, _ = scores_of(st, segc, segl, i)
        st["keep"][i] = keep
        run_t = st["run"][i].T
        parts = []
        for p in range(units // LANES):
            x_pair = block_of(xs_bf, i)[:, p * LANES : (p + 1) * LANES]
            total = None
            for g in range(group):
                tile = (diag * decay_tile(st, i, p * group + g, run_t)).astype(BF16)
                part = mm(tile, x_pair)
                total = part if total is None else jnp.where(lane >= g * per, part, total)
            parts.append(total)
        y = jnp.concatenate(parts, axis=1) + st["skip_u"] * block_of(st["x_act"], i)
        u_i = block_of(st["u_u"], i)
        if i:
            held = jnp.concatenate([c.astype(BF16) for c in carried], axis=0)
            y = y + u_i * mm(off.astype(BF16), held)
        y_ref[i * GROUP : (i + 1) * GROUP, :] = y
        end = u_i[GROUP - 1 : GROUP]
        carried = [c * end for c in carried]
        carried.append(block_of(st["xs"], i) * block_of(st["v_u"], i))


def gate_fwd_kernel(last, mp_count, *refs):
    me, nrm, y, gg, zo = refs[:5]
    at = 5
    if last:
        cot_p = refs[at : at + mp_count]
        at += mp_count
    gate_ref = refs[at]
    outs = refs[at + 1 : at + 1 + mp_count]
    at += 1 + mp_count
    if last:
        stat_ref, dg_ref, up_ref = refs[at : at + 3]
        at += 3
    wz_s, wo_s, po_s = refs[at : at + 3]
    wz = fill_stack(zo, 0, wz_s)
    wo = fill_stack(zo, zo.shape[1] // 2, wo_s)
    gate = mm(nrm[...], wz)
    gate_ref[...] = gate
    mixed = y[...] * (gate * sigmoid(gate))
    weighted = mixed * gg[...]
    squares = jnp.sum(mixed * mixed, axis=1, keepdims=True)
    width = wo.shape[0]
    po_s[:, :width] = mm_nt(weighted.astype(BF16), wo).astype(BF16)
    high, low = high_low(squares)
    rows = squares.shape[0]
    lane = lax.broadcasted_iota(jnp.int32, (rows, LANES), 1)
    extra = jnp.where(lane == 0, high.astype(F32), jnp.where(lane == 1, low.astype(F32), 0.0))
    po_s[:, width:] = extra.astype(BF16)
    own = rows // mp_count
    for q in range(mp_count):
        begin = pl.multiple_of((me[1] ^ q) * own, own)
        outs[q][...] = po_s[pl.ds(begin, own), :]
    if last:
        ups = fill_rows(cot_p, me[1], up_ref)
        if mp_count == 1:
            up_ref[...] = ups
        dg = mm(ups, wo)
        dg_ref[...] = dg
        cross = jnp.sum(dg * weighted, axis=1, keepdims=True)
        stat = jnp.where(lane == 0, squares, jnp.where(lane == 1, cross, 0.0))
        stat_ref[...] = stat.T[:8, :]


def gate_bwd_kernel(last, count, mp_count, inner, *refs):
    me, nrm, y, gate, gg = refs[:5]
    at = 5
    if last:
        stats, dg_in, ups_ref = refs[at : at + 3]
        at += 3
    else:
        ups_p = refs[at : at + mp_count]
        at += mp_count
        zo = refs[at]
        at += 1
    dy_ref, dgate_ref, ggn_ref, out = refs[at : at + 4]
    at += 4
    scratch = refs[at:]
    rows = y.shape[0]
    width = nrm.shape[1]
    if last:
        total = stats[0]
        for k in range(1, stats.shape[0]):
            total = total + stats[k]
        pad = jnp.zeros((LANES - 8, rows), F32)
        cols = jnp.concatenate([total, pad], axis=0).T
        scale = lax.rsqrt(cols[:, 0:1] / inner + EPS)
        kappa = scale * scale * scale * cols[:, 1:2] / inner
        dg = dg_in[...]
        ups = ups_ref[...]
    else:
        ext = fill_rows(ups_p, me[1], scratch[0])
        tail = ext[:, width:].astype(F32)
        scale = tail[:, 0:1] + tail[:, 1:2]
        kappa = tail[:, 2:3] + tail[:, 3:4]
        ups = ext[:, :width]
        wo = fill_stack(zo, zo.shape[1] // 2, scratch[1])
        dg = mm(ups, wo)
    g = gate[...]
    sg = sigmoid(g)
    silu = g * sg
    mixed = y[...] * silu
    scaled = dg * scale
    ggn = jnp.sum(scaled * mixed, axis=0, keepdims=True)
    ggn_ref[...] = jnp.concatenate([ggn, jnp.zeros((7, ggn.shape[1]), F32)], axis=0)
    d_mixed = scaled * gg[...] - mixed * kappa
    d_gate = (d_mixed * y[...] * (sg * (1.0 + g * (1.0 - sg)))).astype(BF16)
    dgate_ref[...] = d_gate
    dy_ref[...] = d_mixed * silu
    gated = (mixed * scale * gg[...]).astype(BF16)
    g_wz = mm_tn(nrm[...], d_gate).astype(BF16)
    g_wo = mm_tn(ups, gated).astype(BF16)
    own = width // count
    for d in range(count):
        out[d, :own, :] = g_wz[d * own : (d + 1) * own]
        out[d, own:, :] = g_wo[d * own : (d + 1) * own]


def mixer_bwd_kernel(heads, count, mp_count, shared, *refs):
    me, nrm, xp, bp, sp, dy_in, dgate, wbc, wdt, cx, cbc, hp, segm, segr, gain, ggn = refs[:16]
    zo, wx = refs[16:18]
    at = 18
    dn_outs = refs[at : at + mp_count]
    at += mp_count
    sm_count = mp_count if shared else 3
    sm_outs = refs[at : at + sm_count]
    at += sm_count
    gx_outs = refs[at : at + count]
    wz_s, dn_s, gw_s, gc_s, gr_s, sm_s, gx_s = refs[at + count :]
    x_pre, bc_pre, stp = xp[...], bp[...], sp[...]
    masks = segm[...]
    segc, segl = masks[:, 3:4], segr[...]
    st = mixer_state(x_pre, bc_pre, stp, cx[...], cbc[...], hp[...], masks, heads)
    st["keep"] = {}
    units, blocks, umap = st["units"], st["blocks"], st["umap"]
    group, per = pair_lanes(heads, units)
    lane = lax.broadcasted_iota(jnp.int32, (GROUP, LANES), 1)
    pos_r = lax.broadcasted_iota(jnp.int32, (GROUP, GROUP), 0)
    pos_c = lax.broadcasted_iota(jnp.int32, (GROUP, GROUP), 1)
    strict = pos_r > pos_c
    upper = jnp.where(pos_c >= pos_r, 1.0, 0.0)
    before = jnp.where(strict, 1.0, 0.0)
    dy = dy_in[...]
    xs_bf = st["xs"].astype(BF16)
    dy_bf = dy.astype(BF16)
    dyu = dy * st["u_u"]
    dyu_bf = dyu.astype(BF16)
    held = [[]]
    for i in range(blocks):
        end = block_of(st["u_u"], i)[GROUP - 1 : GROUP]
        new = [c * end for c in held[i]]
        new.append(block_of(st["xs"], i) * block_of(st["v_u"], i))
        held.append(new)
    later = None
    d_b = [None] * blocks
    d_c = [None] * blocks
    d_xs = [None] * blocks
    d_rate = [None] * blocks
    for i in reversed(range(blocks)):
        off, diag, keep, same = scores_of(st, segc, segl, i)
        st["keep"][i] = keep
        run_t = st["run"][i].T
        d_diag = None
        d_run = None
        parts = []
        for p in range(units // LANES):
            x_pair = block_of(xs_bf, i)[:, p * LANES : (p + 1) * LANES]
            dy_pair = block_of(dy_bf, i)[:, p * LANES : (p + 1) * LANES]
            total = None
            for g in range(group):
                h = p * group + g
                decay = decay_tile(st, i, h, run_t)
                tile = diag * decay
                mine = (lane >= g * per) & (lane < (g + 1) * per)
                d_tile = mm_nt(jnp.where(mine, dy_pair, jnp.zeros_like(dy_pair)), x_pair)
                part = mm_tn(tile.astype(BF16), dy_pair)
                total = part if total is None else jnp.where(lane >= g * per, part, total)
                term = d_tile * decay
                d_diag = term if d_diag is None else d_diag + term
                flow = jnp.where(strict, d_tile * tile, 0.0)
                high, low = high_low(flow)
                pick = jnp.where(pos_c == h, 1.0, 0.0).astype(BF16)
                turn = (mm(high, pick) + mm(low, pick)) - (mm_tn(high, pick) + mm_tn(low, pick))
                d_run = turn if d_run is None else d_run + turn
            parts.append(total)
        grad_xs = jnp.concatenate(parts, axis=1)
        d_scores = d_diag
        direct = None
        if i:
            rows_bf = block_of(dyu_bf, i)
            z_bf = jnp.concatenate([c.astype(BF16) for c in held[i]], axis=0)
            off_bf = off.astype(BF16)
            d_run = d_run + narrow(block_of(dyu, i) * mm(off_bf, z_bf), umap)
            d_off = jnp.where(same[:, : i * GROUP], mm_nt(rows_bf, z_bf), 0.0)
            d_scores = jnp.concatenate([d_off, d_diag], axis=1)
            direct = mm_tn(off_bf, rows_bf)
        rate_grad = jnp.dot(upper, d_run, precision=HIGH, preferred_element_type=F32)
        end = block_of(st["u_u"], i)[GROUP - 1 : GROUP]
        if later is not None:
            into = later[i]
            grad_xs = grad_xs + into * block_of(st["v_u"], i)
            q = narrow(into * held[i + 1][i], umap)
            rate_grad = rate_grad + jnp.dot(before, q, precision=HIGH, preferred_element_type=F32)
            if i:
                through = None
                for j in range(i):
                    part = jnp.sum(later[j] * held[i][j], axis=0, keepdims=True)
                    through = part if through is None else through + part
                through = jnp.broadcast_to(through * end, (8, units))
                rate_grad = rate_grad + narrow(through, umap)[0:1]
        new = []
        for j in range(i):
            term = direct[j * GROUP : (j + 1) * GROUP]
            if later is not None:
                term = term + later[j] * end
            new.append(term)
        later = new
        d_xs[i] = grad_xs
        d_rate[i] = rate_grad
        ds_bf = d_scores.astype(BF16)
        d_c[i] = mm(ds_bf, st["b"][: (i + 1) * GROUP])
        back = mm_tn(ds_bf, block_of(st["c"], i))
        for j in range(i + 1):
            term = back[j * GROUP : (j + 1) * GROUP]
            d_b[j] = term if d_b[j] is None else d_b[j] + term
    d_xs = jnp.concatenate(d_xs, axis=0)
    d_rate = jnp.concatenate(d_rate, axis=0)
    d_bc_act = jnp.concatenate(
        [jnp.concatenate(d_b, axis=0), jnp.concatenate(d_c, axis=0)], axis=1
    )
    d_x_act = d_xs * st["step_u"] + dy * st["skip_u"]
    d_step = narrow(d_xs * st["x_act"], umap) - d_rate * jnp.exp(hp[1:2, :])
    skip_row = jnp.broadcast_to(jnp.sum(dy * st["x_act"], axis=0, keepdims=True), (8, units))
    g_skip = narrow(skip_row, umap)[0:1]
    g_rate = jnp.sum(d_rate * st["rate"], axis=0, keepdims=True)
    d_stp = d_step * sigmoid(st["raw"])
    g_bias = jnp.sum(d_stp, axis=0, keepdims=True)
    head = lax.broadcasted_iota(jnp.int32, d_stp.shape, 1)
    d_stp_bf = jnp.where(head < heads, d_stp, 0.0).astype(BF16)
    d_x, g_cx = conv_back(d_x_act, st["c_x"], x_pre, cx[...], masks)
    d_bc, g_cbc = conv_back(d_bc_act, st["c_bc"], bc_pre, cbc[...], masks)
    d_x_bf = d_x.astype(BF16)
    d_bc_bf = d_bc.astype(BF16)
    wz = fill_stack(zo, 0, wz_s)
    dn = mm_nt(dgate[...], wz) + mm_nt(d_x_bf, wx[...])
    dn = dn + mm_nt(d_stp_bf, wdt[...]) + mm_nt(d_bc_bf, wbc[...])
    normed = nrm[...]
    hnorm = normed.astype(F32) / gain[...]
    g_gain = jnp.sum(dn * hnorm, axis=0, keepdims=True)
    width = normed.shape[1]
    rows = normed.shape[0]
    dn_s[...] = dn.astype(BF16)
    own = rows // mp_count
    for q in range(mp_count):
        begin = pl.multiple_of((me[1] ^ q) * own, own)
        dn_outs[q][...] = dn_s[pl.ds(begin, own), :]
    bc_units = d_bc.shape[1]
    gw_s[...] = mm_tn(normed, d_bc_bf)
    none = jnp.zeros((7, width), F32)
    g_high = g_gain.astype(BF16).astype(F32)
    gain_rows = jnp.concatenate(
        [g_high, none, g_gain - g_high, none, jnp.zeros((LANES - 16, width), F32)], axis=0
    )
    gr_s[...] = gain_rows.T
    c_high = g_cbc.astype(BF16).astype(F32)
    conv_rows = jnp.concatenate([c_high, g_cbc - c_high, jnp.zeros((LANES - 16, bc_units), F32)], axis=0)
    gc_s[...] = conv_rows.T
    if shared:
        w_own = width // (shared * mp_count)
        c_own = bc_units // (shared * mp_count)
        for q in range(mp_count):
            for k in range(shared):
                slot = k * mp_count + (me[1] ^ q)
                sm_s[k * w_own : (k + 1) * w_own, :] = gw_s[
                    pl.ds(pl.multiple_of(slot * w_own, 8), w_own), :
                ]
                base = shared * w_own + k * c_own
                tile = gc_s[pl.ds(pl.multiple_of(slot * c_own, 8), c_own), :]
                for c in range(w_own // 8):
                    part = gr_s[pl.ds(pl.multiple_of(slot * w_own + 8 * c, 8), 8), :]
                    tile = tile + pltpu.roll(part, 16 + c, 1)
                sm_s[base : base + c_own, :LANES] = tile
                sm_s[base : base + c_own, LANES:] = jnp.zeros((c_own, bc_units - LANES), F32)
            sm_outs[q][...] = sm_s[...].astype(BF16)
    else:
        sm_outs[0][...] = gw_s[...]
        sm_outs[1][...] = gc_s[...]
        sm_outs[2][...] = gr_s[...]
    gx_s[...] = mm_tn(normed, d_x_bf).astype(BF16)
    heads_row = jnp.concatenate([g_bias, g_rate, g_skip], axis=1)
    if heads_row.shape[1] < units:
        heads_row = jnp.concatenate(
            [heads_row, jnp.zeros((1, units - heads_row.shape[1]), F32)], axis=1
        )
    small = jnp.concatenate([g_cx[:5], ggn[0:1, :], heads_row, jnp.zeros((1, units), F32)], axis=0)
    s_high, s_low = high_low(small)
    g_dt = mm_tn(d_stp_bf, normed)[:8]
    halves = [g_dt[:, k * units : (k + 1) * units] for k in range(width // units)]
    tail = jnp.concatenate([s_high.astype(F32), s_low.astype(F32)] + halves, axis=0).astype(BF16)
    own = width // count
    for k in range(count):
        begin = pl.multiple_of((me[0] ^ k) * own, own)
        gx_outs[k][:own, :] = gx_s[pl.ds(begin, own), :]
        gx_outs[k][own:, :] = tail


def after_fwd_kernel(last, mp_count, inner, *refs):
    parts = refs[:mp_count]
    hidden, gain = refs[mp_count : mp_count + 2]
    outs = refs[mp_count + 2 :]
    total = parts[0][...].astype(F32)
    for part in parts[1:]:
        total = total + part[...].astype(F32)
    width = hidden.shape[1]
    squares = total[:, width : width + 1] + total[:, width + 1 : width + 2]
    scale = lax.rsqrt(squares / inner + EPS)
    branch = total[:, :width] * scale
    new = hidden[...] + branch
    outs[0][...] = new
    if not last:
        norm = lax.rsqrt(jnp.mean(new * new, axis=1, keepdims=True) + EPS)
        outs[1][...] = (new * norm * gain[...]).astype(BF16)
        outs[2][...] = branch
        outs[3][...] = scale


def after_bwd_kernel(first, mp_count, inner, *refs):
    parts = refs[:mp_count]
    at = mp_count
    ups, hidden, gain = refs[at : at + 3]
    at += 3
    if not first:
        branch, gscale = refs[at : at + 2]
        at += 2
    up_ref = refs[at]
    at += 1
    if not first:
        ext_ref = refs[at]
        at += 1
    h = hidden[...]
    width = h.shape[1]
    dn = parts[0][:, :width].astype(F32)
    for part in parts[1:]:
        dn = dn + part[:, :width].astype(F32)
    scale = lax.rsqrt(jnp.mean(h * h, axis=1, keepdims=True) + EPS)
    hnorm = h * scale
    dh = dn * gain[...]
    new = ups[...] + scale * (dh - hnorm * jnp.mean(dh * hnorm, axis=1, keepdims=True))
    up_ref[...] = new
    if not first:
        rounded = new.astype(BF16)
        gs = gscale[...]
        dot = jnp.sum(rounded.astype(F32) * branch[...], axis=1, keepdims=True)
        kappa = gs * gs * dot / inner
        lane = lax.broadcasted_iota(jnp.int32, (h.shape[0], LANES), 1)
        s_high, s_low = high_low(gs)
        k_high, k_low = high_low(kappa)
        extra = jnp.zeros((h.shape[0], LANES), F32)
        for at_lane, col in enumerate((s_high, s_low, k_high, k_low)):
            extra = jnp.where(lane == at_lane, col.astype(F32), extra)
        ext_ref[:, :width] = rounded
        ext_ref[:, width:] = extra.astype(BF16)


def shared_kernel(layers, mp_count, count, *refs):
    me, parts = refs[0], refs[1 : 1 + layers * mp_count]
    outs = refs[1 + layers * mp_count : -1]
    total_s = refs[-1]
    rows = total_s.shape[0]
    w_rows = rows * 3 // 4
    w_own, c_own = w_rows // count, (rows - w_rows) // count
    for layer in range(layers):
        mine = parts[layer * mp_count : (layer + 1) * mp_count]
        total = mine[0][...].astype(F32)
        for part in mine[1:]:
            total = total + part[...].astype(F32)
        total_s[:w_rows, :] = total[:w_rows]
        tile = total[w_rows:, :LANES]
        lane = lax.broadcasted_iota(jnp.int32, tile.shape, 1)
        joined = jnp.where((lane & 8) == 0, tile + pltpu.roll(tile, LANES - 8, 1), 0.0)
        high = joined.astype(BF16).astype(F32)
        total_s[w_rows:, :LANES] = high + pltpu.roll(joined - high, 8, 1)
        total_s[w_rows:, LANES:] = jnp.zeros((rows - w_rows, total.shape[1] - LANES), F32)
        base = layer * (w_own + c_own)
        for k in range(count):
            slot = me[0] ^ k
            top = total_s[pl.ds(pl.multiple_of(slot * w_own, 8), w_own), :]
            low = total_s[pl.ds(pl.multiple_of(w_rows + slot * c_own, 8), c_own), :]
            both = jnp.concatenate([top, low], axis=0).astype(BF16)
            outs[k][base : base + w_own + c_own, :] = both


def place_kernel(*refs):
    me, pieces, (wx_ref, sm_ref) = refs[0], refs[1:-2], refs[-2:]
    rows = wx_ref.shape[0] // len(pieces)
    half = rows // 2
    left = pieces[0].shape[1]
    rest = wx_ref.shape[1] - left
    sm_rows = pieces[0].shape[0] - rows - half
    for k, piece in enumerate(pieces):
        at = pl.multiple_of((me[0] ^ k) * rows, half)
        below = pl.multiple_of(at + half, half)
        wx_ref[pl.ds(at, rows), :left] = piece[:rows, :]
        wx_ref[pl.ds(at, half), left:] = piece[rows : rows + half, :rest]
        wx_ref[pl.ds(below, half), left:] = piece[rows : rows + half, rest:]
        at = pl.multiple_of((me[0] ^ k) * sm_rows, sm_rows)
        sm_ref[pl.ds(at, sm_rows), :] = piece[rows + half :, :]


def small_kernel(layers, taps, dt_groups, own_w, mp_count, *refs):
    me = refs[0]
    every = refs[1 : 1 + mp_count]
    hs = refs[1 + mp_count : 1 + 2 * mp_count]
    wbc_ref, wdt_ref, gain_ref, cbc_ref, nrm_ref = refs[1 + 2 * mp_count : 6 + 2 * mp_count]
    w_s, g_s, c_s, d_s = refs[6 + 2 * mp_count :]
    mine = every[0]
    dp_count = mine.shape[0] // (layers * (own_w + 8))
    for layer in range(layers):
        d_s[...] = jnp.zeros(d_s.shape, F32)
        for d in range(dp_count):
            base = (d * layers + layer) * (own_w + 8)
            for q in range(mp_count):
                slot = d * mp_count + (me[1] ^ q)
                row = pl.multiple_of(slot * own_w, 8)
                w_s[pl.ds(row, own_w), :] = every[q][base : base + own_w, :].astype(F32)
                tile = every[q][base + own_w - 8 : base + own_w + 8, :LANES].astype(F32)[8:]
                c_s[pl.ds(pl.multiple_of(slot * 8, 8), 8), :] = tile
                for c in range(own_w // 8):
                    row = pl.multiple_of(slot * own_w + 8 * c, 8)
                    g_s[pl.ds(row, 8), :] = pltpu.roll(tile, LANES - 8 - c, 1)
            tile = mine[base + own_w - 8 : base + own_w + 8, :LANES].astype(F32)[8:]
            for g in range(dt_groups):
                row = (d * dt_groups + g) * 8
                d_s[row : row + 8, :] = pltpu.roll(tile, LANES - 16 - 8 * g, 1)
        wbc_ref[layer] = w_s[...].astype(BF16)
        lane = lax.broadcasted_iota(jnp.int32, d_s.shape, 1)
        wdt_ref[layer] = jnp.where(lane < 8, d_s[...], 0.0).astype(BF16)
        gain = g_s[...].T[:8]
        gain_ref[layer] = gain
        conv = c_s[...].T[:8]
        row = lax.broadcasted_iota(jnp.int32, conv.shape, 0)
        cbc_ref[layer] = jnp.where(row < taps, conv, 0.0)
        if layer == 0:
            rows = hs[0].shape[0]
            for q in range(mp_count):
                at = pl.multiple_of((me[1] ^ q) * rows, rows)
                nrm_ref[pl.ds(at, rows), :] = (hs[q][...].astype(F32) * gain[0:1]).astype(BF16)


def call(kernel, name, inputs, outputs, scratch=(), flops=1 << 28):
    specs = []
    for value in inputs:
        space = pltpu.SMEM if value.dtype == jnp.int32 and value.ndim == 1 else pltpu.VMEM
        specs.append(pl.BlockSpec(memory_space=space))
    size = sum(v.size * v.dtype.itemsize for v in inputs)
    size += sum(v.size * v.dtype.itemsize for v in outputs)
    return pl.pallas_call(
        kernel,
        out_shape=[jax.ShapeDtypeStruct(o.shape, o.dtype) for o in outputs],
        in_specs=specs,
        out_specs=[pl.BlockSpec(memory_space=pltpu.VMEM) for _ in outputs],
        scratch_shapes=list(scratch),
        cost_estimate=pl.CostEstimate(flops=flops, bytes_accessed=size, transcendentals=0),
        compiler_params=pltpu.CompilerParams(vmem_limit_bytes=60 << 20),
        interpret=INTERPRET,
        name=name,
    )(*inputs)


def shape(dims, dtype):
    return jax.ShapeDtypeStruct(tuple(dims), dtype)


def partners(axis, k):
    return [(i, i ^ k) for i in range(lax.axis_size(axis))]


def spread(value, axis):
    n = lax.axis_size(axis)
    return [value] + [lax.ppermute(value, axis, partners(axis, k)) for k in range(1, n)]


def exchange(values, axis):
    n = lax.axis_size(axis)
    return [values[0]] + [lax.ppermute(values[k], axis, partners(axis, k)) for k in range(1, n)]


def share(value, axis):
    n = lax.axis_size(axis)
    return lax.all_to_all(jnp.broadcast_to(value[None], (n,) + value.shape), axis, 0, 0)


def swap(stack, axis):
    return lax.all_to_all(stack, axis, 0, 0)


def add_up(stack):
    if isinstance(stack, (list, tuple)):
        total = stack[0].astype(F32)
        for piece in stack[1:]:
            total = total + piece.astype(F32)
        return total
    return jnp.sum(stack.astype(F32), axis=0)


def after(value, *others):
    return lax.optimization_barrier((value,) + others)[0]


def body(
    h_in,
    w_z,
    w_x,
    w_bc,
    w_dt,
    w_out,
    conv_x,
    conv_bc,
    dt_bias,
    a_log,
    d_skip,
    rms_gain,
    gnorm_gain,
    seg_ids,
    cotangent,
):
    dp, mp = lax.axis_size("dp"), lax.axis_size("mp")
    direct = dp & (dp - 1) == 0 and conv_bc.shape[2] == 8 and w_bc.shape[1] == 24
    layers, width_own, units = w_z.shape
    width = h_in.shape[1]
    tokens = h_in.shape[0] * mp
    own = h_in.shape[0]
    heads = w_dt.shape[2]
    bc_units = w_bc.shape[2]
    taps = conv_x.shape[1]
    inner = units * mp
    my_dp, my_mp = lax.axis_index("dp"), lax.axis_index("mp")
    me = jnp.stack([my_dp if direct else jnp.zeros_like(my_dp), my_mp]).astype(jnp.int32)
    count = dp if direct else 1
    w_rows = width // count

    out_t = jnp.swapaxes(w_out, 1, 2)
    hidden = h_in
    scale = lax.rsqrt(jnp.mean(h_in * h_in, axis=1, keepdims=True) + EPS)
    scaled = (h_in * scale).astype(BF16)
    wx_full, zo_full = [], []
    if direct:
        own_w = w_bc.shape[1]
        own_c = conv_bc.shape[2]
        groups = width_own // 8
        dt = jnp.pad(w_dt, ((0, 0), (0, 0), (0, 8 - heads))).reshape(layers, groups, 8, 8)
        dt = jnp.swapaxes(dt, 1, 2).reshape(layers, 8, groups * 8)
        gain = jnp.swapaxes(rms_gain.reshape(layers, own_w // 8, 8), 1, 2)
        conv = jnp.pad(jnp.swapaxes(conv_bc, 1, 2), ((0, 0), (0, 0), (0, 8 - taps)))
        low = jnp.concatenate([conv, jnp.pad(gain, ((0, 0), (0, 0), (0, 8 - own_w // 8))), dt], axis=2)
        low = jnp.pad(low, ((0, 0), (0, 0), (0, bc_units - low.shape[2])))
        packed = jnp.concatenate([w_bc, low], axis=1).reshape(-1, bc_units)
        half = width_own // 2
        first = w_x[0]
        group = jnp.concatenate(
            [
                first[:, :bc_units],
                jnp.concatenate([first[:half, bc_units:], first[half:, bc_units:]], axis=1),
                packed,
            ],
            axis=0,
        )
        pieces = spread(group, "dp")
        wx0, mine = call(
            place_kernel,
            "place",
            [me] + pieces,
            [shape((width, units), BF16), shape((dp * packed.shape[0], bc_units), BF16)],
        )
        wx_full.append([wx0])
        hs = spread(scaled, "mp")
        every = spread(mine, "mp")
        wbc, wdt, gains, cbc, normed = call(
            partial(small_kernel, layers, taps, groups, own_w, mp),
            "small",
            [me] + every + hs,
            [
                shape((layers, width, bc_units), BF16),
                shape((layers, width, LANES), BF16),
                shape((layers, 8, width), F32),
                shape((layers, 8, bc_units), F32),
                shape((tokens, width), BF16),
            ],
            [
                pltpu.VMEM((width, bc_units), F32),
                pltpu.VMEM((width, LANES), F32),
                pltpu.VMEM((bc_units, LANES), F32),
                pltpu.VMEM((width, LANES), F32),
            ],
        )
        gains = gains[:, 0]
        zo_own = [jnp.concatenate([w_z[layer], out_t[layer]], axis=0) for layer in range(layers)]
        zo_full.append(share(zo_own[0], "dp"))
    else:
        both = ("dp", "mp")
        wbc = lax.all_gather(w_bc, both, axis=1, tiled=True)
        gains = lax.all_gather(rms_gain, both, axis=1, tiled=True).astype(F32)
        cbc = lax.all_gather(conv_bc, both, axis=2, tiled=True).astype(F32)
        cbc = jnp.pad(cbc, ((0, 0), (0, 8 - taps), (0, 0)))
        wdt = lax.all_gather(w_dt, "dp", axis=1, tiled=True)
        wdt = jnp.pad(wdt, ((0, 0), (0, 0), (0, LANES - heads)))
        for layer in range(layers):
            wx_full.append([lax.all_gather(w_x[layer], "dp", axis=0, tiled=True)])
            pair = [
                lax.all_gather(value, "dp", axis=0, tiled=True)
                for value in (w_z[layer], out_t[layer])
            ]
            zo_full.append(jnp.concatenate(pair, axis=0)[None])
        hs = lax.all_gather(scaled, "mp", axis=0, tiled=True)
        normed = (hs.astype(F32) * gains[0][None, :]).astype(BF16)
    normed = [normed]

    segment = seg_ids[0]
    seg_f = segment.astype(F32)
    cols = []
    for offset in range(1, 4):
        earlier = jnp.concatenate([jnp.full((offset,), -1, jnp.int32), segment[:-offset]])
        cols.append((earlier == segment).astype(F32))
    segm = jnp.stack(cols + [seg_f], axis=1)
    segr = seg_f[None, :]
    hp = jnp.stack([dt_bias, a_log, d_skip], axis=1)
    hp = jnp.pad(hp, ((0, 0), (0, 5), (0, LANES - heads)))
    cx = jnp.pad(conv_x, ((0, 0), (0, 8 - taps), (0, 0)))

    cot_p = spread(cotangent.astype(BF16), "mp")

    saved = []
    for layer in range(layers):
        last = layer == layers - 1
        with jax.named_scope(f"fwd_{layer}"):
            outs = [
                shape((tokens, units), F32),
                shape((tokens, bc_units), F32),
                shape((tokens, LANES), F32),
                shape((tokens, units), F32),
            ]
            if len(normed) > 1:
                outs.append(shape((tokens, width), BF16))
            if len(wx_full[layer]) > 1:
                outs.append(shape((width, units), BF16))
            res = call(
                partial(mixer_fwd_kernel, heads, len(normed), len(wx_full[layer])),
                "mixer_fwd",
                [me, wbc[layer], wdt[layer], cx[layer], cbc[layer], hp[layer], segm, segr]
                + normed
                + wx_full[layer],
                outs,
                flops=8 << 30,
            )
            x_pre, bc_pre, stp, y = res[:4]
            if len(wx_full[layer]) > 1:
                wx_full[layer] = [res[-1]]
            normed = res[4] if len(normed) > 1 else normed[0]
            if direct and not last:
                zo_full.append(share(after(zo_own[layer + 1], y), "dp"))
            gg = gnorm_gain[layer][None, :]
            outs = [shape((tokens, units), F32)]
            outs += [shape((own, width + LANES), BF16)] * mp
            ins = [me, normed, y, gg, zo_full[layer]]
            if last:
                ins += cot_p
                outs += [
                    shape((8, tokens), F32),
                    shape((tokens, units), F32),
                    shape((tokens, width), BF16),
                ]
            res = call(
                partial(gate_fwd_kernel, last, mp),
                "gate_fwd",
                ins,
                outs,
                [
                    pltpu.VMEM((width, units), BF16),
                    pltpu.VMEM((width, units), BF16),
                    pltpu.VMEM((tokens, width + LANES), BF16),
                ],
                flops=4 << 30,
            )
            gate, parts = res[0], res[1 : 1 + mp]
            if direct and not last:
                wx_full.append(spread(after(w_x[layer + 1], gate), "dp"))
            if last:
                stats = lax.all_gather(res[1 + mp], "mp", axis=0)
                dg, ups_bf = res[2 + mp], res[3 + mp]
            got = exchange(parts, "mp")
            keep = dict(hidden=hidden, normed=normed, x_pre=x_pre, bc_pre=bc_pre, stp=stp, y=y, gate=gate, gg=gg)
            nxt = gains[min(layer + 1, layers - 1)][None, :]
            outs = [shape((own, width), F32)]
            if not last:
                outs += [
                    shape((own, width), BF16),
                    shape((own, width), F32),
                    shape((own, 1), F32),
                ]
            res = call(
                partial(after_fwd_kernel, last, mp, float(inner)),
                "after_fwd",
                got + [hidden, nxt],
                outs,
                flops=1 << 28,
            )
            hidden = res[0]
            if not last:
                keep["branch"], keep["gscale"] = res[2], res[3]
                normed = spread(res[1], "mp")
            saved.append(keep)

    upstream = cotangent
    results = [None] * layers
    ext_p = None
    shared = dp if direct else 0
    sm_rows = (width + bc_units) // mp
    sm_parts = [None] * layers
    sums = [None] * layers
    for layer in reversed(range(layers)):
        last = layer == layers - 1
        keep = saved[layer]
        with jax.named_scope(f"bwd_{layer}"):
            y_in = keep["y"]
            if direct and not last:
                y_in = after(y_in, sums[layer + 1][0])
            ins = [me, keep["normed"], y_in, keep["gate"], keep["gg"]]
            scratch = []
            if last:
                ins += [stats, dg, ups_bf]
            else:
                ins += ext_p + [zo_full[layer]]
                scratch += [
                    pltpu.VMEM((tokens, width + LANES), BF16),
                    pltpu.VMEM((width, units), BF16),
                ]
            res = call(
                partial(gate_bwd_kernel, last, count, mp, float(inner)),
                "gate_bwd",
                ins,
                [
                    shape((tokens, units), F32),
                    shape((tokens, units), BF16),
                    shape((8, units), F32),
                ]
                + [shape((count, 2 * w_rows, units), BF16)],
                scratch,
                flops=6 << 30,
            )
            dy, dgate, ggn, zo_grads = res
            zo_sum = add_up(swap(zo_grads, "dp")) if direct else zo_grads
            outs = [shape((own, width), BF16)] * mp
            if shared:
                outs += [shape((sm_rows, bc_units), BF16)] * mp
            else:
                outs += [
                    shape((width, bc_units), F32),
                    shape((bc_units, LANES), F32),
                    shape((width, LANES), F32),
                ]
            tail_rows = 16 + 8 * (width // units)
            outs += [shape((w_rows + tail_rows, units), BF16)] * count
            res = call(
                partial(mixer_bwd_kernel, heads, count, mp, shared),
                "mixer_bwd",
                [
                    me, keep["normed"], keep["x_pre"], keep["bc_pre"], keep["stp"], dy, dgate,
                    wbc[layer], wdt[layer], cx[layer], cbc[layer], hp[layer], segm, segr,
                    gains[layer][None, :], ggn, zo_full[layer], wx_full[layer][0],
                ],
                outs,
                [
                    pltpu.VMEM((width, units), BF16),
                    pltpu.VMEM((tokens, width), BF16),
                    pltpu.VMEM((width, bc_units), F32),
                    pltpu.VMEM((bc_units, LANES), F32),
                    pltpu.VMEM((width, LANES), F32),
                    pltpu.VMEM((sm_rows, bc_units), F32),
                    pltpu.VMEM((width, units), BF16),
                ],
                flops=16 << 30,
            )
            dn_parts = exchange(res[:mp], "mp")
            if shared:
                sm_parts[layer] = exchange(res[mp : 2 * mp], "mp")
                gx = add_up(exchange(res[2 * mp :], "dp"))
            else:
                sm_parts[layer] = res[mp : mp + 3]
                gx = res[mp + 3]
            sums[layer] = (zo_sum, gx)
            ins = dn_parts + [upstream, keep["hidden"], gains[layer][None, :]]
            outs = [shape((own, width), F32)]
            first = layer == 0
            if not first:
                ins += [saved[layer - 1]["branch"], saved[layer - 1]["gscale"]]
                outs += [shape((own, width + LANES), BF16)]
            res = call(
                partial(after_bwd_kernel, first, mp, float(inner)),
                "after_bwd",
                ins,
                outs,
                flops=1 << 28,
            )
            upstream = res[0]
            if not first:
                ext_p = spread(res[1], "mp")
    if direct:
        own_w = w_bc.shape[1]
        sm_own = own_w + conv_bc.shape[2]
        parts = call(
            partial(shared_kernel, layers, mp, count),
            "shared_sums",
            [me] + [part for group in sm_parts for part in group],
            [shape((layers * sm_own, bc_units), BF16)] * count,
            [pltpu.VMEM((sm_rows, bc_units), F32)],
        )
        sm_all = add_up(exchange(parts, "dp")).reshape(layers, sm_own, bc_units)
    for layer in range(layers):
        zo, gx = sums[layer]
        if direct:
            sm = sm_all[layer]
            g_wbc = sm[:own_w]
            low = sm[own_w:, :32]
            low = (low + jnp.roll(low, -8, axis=1)).T
            g_cbc = low[:taps]
            g_gain = low[16 : 16 + own_w // 8].reshape(-1)
            g_wz, g_wo = zo[:w_rows], zo[w_rows:].T
            g_wx, tail = gx[:w_rows], gx[w_rows:]
        else:

            def scattered(value, axes="dp"):
                return lax.psum_scatter(value.astype(F32), axes, scatter_dimension=0, tiled=True)

            g_wz = scattered(zo[0, :width])
            g_wo = scattered(zo[0, width:]).T
            g_wx = scattered(gx[:width])
            tail = lax.psum(gx[width:].astype(F32), "dp")
            g_wbc = scattered(sm_parts[layer][0], ("dp", "mp"))
            gc = scattered(sm_parts[layer][1], ("dp", "mp"))
            gr = scattered(sm_parts[layer][2], ("dp", "mp"))
            g_gain = gr[:, 0] + gr[:, 8]
            g_cbc = (gc[:, :taps] + gc[:, 8 : 8 + taps]).T
        small = tail[:8] + tail[8:16]
        g_dt = jnp.concatenate(
            [tail[16 + 8 * k : 24 + 8 * k] for k in range(width // units)], axis=1
        )
        g_dt = lax.dynamic_slice_in_dim(g_dt[:heads], my_dp * width_own, width_own, 1).T
        results[layer] = (
            g_wz,
            g_wx,
            g_wbc,
            g_dt,
            g_wo,
            small[:taps],
            g_cbc,
            small[6, :heads],
            small[6, LANES : LANES + heads],
            small[6, 2 * LANES : 2 * LANES + heads],
            g_gain,
            small[5],
        )
    stacked = [jnp.stack([results[i][m] for i in range(layers)]) for m in range(12)]
    return tuple([hidden, upstream] + stacked)


def solution(mesh):
    placed = (
        P(("dp", "mp"), None),
        P(None, "dp", "mp"),
        P(None, "dp", "mp"),
        P(None, ("dp", "mp"), None),
        P(None, "dp", "mp"),
        P(None, "mp", "dp"),
        P(None, None, "mp"),
        P(None, None, ("dp", "mp")),
        P(None, "mp"),
        P(None, "mp"),
        P(None, "mp"),
        P(None, ("dp", "mp")),
        P(None, "mp"),
        P("dp", None),
        P(("dp", "mp"), None),
    )
    return jax.shard_map(
        body,
        mesh=mesh,
        in_specs=placed,
        out_specs=(
            P(("dp", "mp"), None),
            P(("dp", "mp"), None),
            P(None, "dp", "mp"),
            P(None, "dp", "mp"),
            P(None, ("dp", "mp"), None),
            P(None, "dp", "mp"),
            P(None, "mp", "dp"),
            P(None, None, "mp"),
            P(None, None, ("dp", "mp")),
            P(None, "mp"),
            P(None, "mp"),
            P(None, "mp"),
            P(None, ("dp", "mp")),
            P(None, "mp"),
        ),
        check_vma=False,
    )
```
